256 devices in a mesh: dp: 64 (over z, x, core), mp: 4 (over y).
Axes of the slice: x: 4, y: 4, z: 8, core: 2. Of those that a mesh axis runs over, the one named last changes fastest.
Arguments:
- hidden: bfloat16 [64, 512, 4608], P('dp', 'mp'), may hold values from -6 to 6
- lengths: int32 [64], P('dp'), may hold values from 64 to 512
- norm_gain: float32 [4608], replicated, may hold values from 0.25 to 1.75
- w_query: bfloat16 [4608, 2048], P('dp', 'mp'), may hold values from -0.09375 to 0.09375
- w_key: bfloat16 [4608, 1024], P('dp', 'mp'), may hold values from -0.09375 to 0.09375
- w_value: bfloat16 [4608, 1024], P('dp', 'mp'), may hold values from -0.09375 to 0.09375
- w_out: bfloat16 [2048, 4608], P('mp', 'dp'), may hold values from -0.125 to 0.125
- post_gain: float32 [4608], replicated, may hold values from 0.25 to 1.75
Outputs:
- mixed: bfloat16 [64, 512, 4608], P('dp', 'mp')
- key_cache: bfloat16 [64, 512, 1024], P('dp', None, 'mp')
- value_cache: bfloat16 [64, 512, 1024], P('dp', None, 'mp')
The draws below stay inside these ranges and needn't reach their ends.
All inputs are finite; a program needn't handle non-finite values.
Results may differ from the reference program's by a relative error of at most 0.01.
Values may be sent and summed in bfloat16 or wider, within the bound.
No kernel may reach another device: no remote copies, remote signals or barrier semaphores. Data moves between devices by JAX's collectives and lax.ppermute only.
A program may use at most 128 MiB of HBM per device.

```python
import jax
import jax.numpy as jnp
from jax import lax

D = 4608
HD = 128
QH = 16
KVH = 8
MAXLEN = 512
MINLEN = 64
ROLLOUTS = 64
N_MP = 4


def place_ends(values, key, low, largest):
    spot = [jax.random.randint(jax.random.fold_in(key, axis), (), 0, length) for axis, length in enumerate(values.shape)]
    widest = values.shape.index(max(values.shape))
    beside = spot[:widest] + [(spot[widest] + 1) % values.shape[widest]] + spot[widest + 1:]
    return values.at[tuple(spot)].set(low).at[tuple(beside)].set(largest)


def block_levels(own_key, shape, pieces, least, largest):
    level, own = 1.0, jax.random.fold_in(own_key, 6)
    for position, shards_of in pieces:
        steps = jnp.exp(jax.random.uniform(jax.random.fold_in(own, position), (shards_of,), jnp.float32, least / len(pieces), largest / len(pieces)))
        level = level * jnp.repeat(steps, shape[position] // shards_of).reshape([-1 if axis == position else 1 for axis in range(len(shape))])
    return level


def centred(stream_key, shape, scale, limit, cuts=(), kind=jnp.bfloat16):
    result = scale * jax.random.normal(stream_key, shape, jnp.float32)
    if cuts:
        result = result * block_levels(stream_key, shape, cuts, -0.22, 0.18)
    return jnp.clip(result, -limit, limit).astype(kind)


def setup_inputs(seed: int = 0) -> dict:
    seeds = jax.random.split(jax.random.key(seed), 9)
    hidden = centred(seeds[0], (ROLLOUTS, MAXLEN, D), 1.0, 6.0, ((0, 64), (1, 4)))
    lengths = place_ends(jax.random.randint(seeds[1], (ROLLOUTS,), MINLEN, MAXLEN + 1), jax.random.fold_in(seeds[1], 1), MINLEN, MAXLEN).astype(jnp.int32)
    norm_gain = jnp.clip(1.0 + 0.15 * jax.random.normal(seeds[2], (D,), jnp.float32), 0.25, 1.75)
    w_query = centred(seeds[3], (D, QH * HD), D ** -0.5, 0.09375, ((0, 64), (1, 4)))
    w_key = centred(seeds[4], (D, KVH * HD), D ** -0.5, 0.09375, ((0, 64), (1, 4)))
    w_value = centred(seeds[5], (D, KVH * HD), D ** -0.5, 0.09375, ((0, 64), (1, 4)))
    w_out = centred(seeds[6], (QH * HD, D), (QH * HD) ** -0.5, 0.125, ((0, 4), (1, 64)))
    post_gain = jnp.clip(1.0 + 0.15 * jax.random.normal(seeds[7], (D,), jnp.float32), 0.25, 1.75)
    return {"hidden": hidden, "lengths": lengths, "norm_gain": norm_gain, "w_query": w_query, "w_key": w_key, "w_value": w_value, "w_out": w_out, "post_gain": post_gain}


def rotate(values, positions):
    half = values.shape[-1] // 2
    freqs = 10000.0 ** (-jnp.arange(half, dtype=jnp.float32) / half)
    angles = positions.astype(jnp.float32)[:, None] * freqs[None, :]
    cosine = jnp.cos(angles)[:, None, :]
    sine = jnp.sin(angles)[:, None, :]
    first = values[..., :half]
    second = values[..., half:]
    return jnp.concatenate([first * cosine - second * sine, second * cosine + first * sine], axis=-1)

def one_rollout(args, norm_gain, w_query, w_key, w_value, w_out, post_gain):
    rows, length = args
    maxlen = rows.shape[0]
    group = QH // KVH
    rows_f = rows.astype(jnp.float32)
    normed = (rows_f * lax.rsqrt(lax.optimization_barrier(jnp.mean(rows_f * rows_f, axis=-1, keepdims=True)) + 1e-06) * norm_gain).astype(jnp.bfloat16)
    positions = jnp.arange(maxlen, dtype=jnp.int32)
    qraw = jnp.dot(normed, w_query, preferred_element_type=jnp.float32).reshape(maxlen, QH, HD)
    kraw = jnp.dot(normed, w_key, preferred_element_type=jnp.float32).reshape(maxlen, KVH, HD)
    vraw = jnp.dot(normed, w_value, preferred_element_type=jnp.float32).reshape(maxlen, KVH, HD)
    query = (rotate(qraw, positions) * 144.0 ** (-0.5)).astype(jnp.bfloat16)
    key = rotate(kraw, positions).astype(jnp.bfloat16)
    value = vraw.astype(jnp.bfloat16)
    grouped = query.reshape(maxlen, KVH, group, HD).astype(jnp.float32)
    score = jnp.einsum('qkgd,tkd->kgqt', grouped, key.astype(jnp.float32))
    score = 50.0 * jnp.tanh(score / 50.0)
    keep = (positions[None, :] <= positions[:, None]) & (positions[None, :] < length)
    score = jnp.where(keep[None, None], score, -1e+30)
    top = lax.optimization_barrier(jnp.max(score, axis=-1, keepdims=True))
    expo = jnp.exp(score - top)
    weights = (expo / lax.optimization_barrier(jnp.sum(expo, axis=-1, keepdims=True))).astype(jnp.bfloat16)
    attended = jnp.einsum('kgqt,tkd->qkgd', weights.astype(jnp.float32), value.astype(jnp.float32))
    attended = attended.reshape(maxlen, QH * HD).astype(jnp.bfloat16)
    cols = QH * HD // N_MP
    projected = jnp.zeros((maxlen, D), jnp.float32)
    for part in range(N_MP):
        partial_value = jnp.dot(attended[:, part * cols:(part + 1) * cols], w_out[part * cols:(part + 1) * cols], preferred_element_type=jnp.float32)
        projected = projected + partial_value.astype(jnp.bfloat16).astype(jnp.float32)
    post = projected * lax.rsqrt(lax.optimization_barrier(jnp.mean(projected * projected, axis=-1, keepdims=True)) + 1e-06) * post_gain
    live = (positions < length)[:, None]
    mixed = jnp.where(live, rows_f + post, 0.0).astype(jnp.bfloat16)
    key_rows = jnp.where(live, key.reshape(maxlen, KVH * HD), jnp.zeros((), jnp.bfloat16))
    value_rows = jnp.where(live, value.reshape(maxlen, KVH * HD), jnp.zeros((), jnp.bfloat16))
    return (mixed, key_rows, value_rows)

def reference(hidden, lengths, norm_gain, w_query, w_key, w_value, w_out, post_gain):

    def step(args):
        return one_rollout(args, norm_gain, w_query, w_key, w_value, w_out, post_gain)
    mixed, key_cache, value_cache = lax.map(step, (hidden, lengths))
    return (mixed, key_cache, value_cache)
```

```python
import functools

import jax
import jax.numpy as jnp
from jax import lax
from jax.experimental import pallas as pl
from jax.experimental.pallas import tpu as pltpu
from jax.sharding import PartitionSpec as P


HD = 128
NZ, NX, NY = 8, 4, 4
F32 = jnp.float32
BF16 = jnp.bfloat16
ANY = pl.BlockSpec(memory_space=pl.ANY)
SMALL_LIMIT = 24 * 1024 * 1024


def spot(z, x, c):
    return ((z % NZ) * NX + (x % NX)) * 2 + c


def plane(array, dz=0, dx=0, dc=0):
    pairs = [
        (spot(z, x, c), spot(z + dz, x + dx, c ^ dc))
        for z in range(NZ)
        for x in range(NX)
        for c in range(2)
    ]
    return lax.ppermute(array, "dp", pairs)


def column(array, dy):
    return lax.ppermute(array, "mp", [(y, (y + dy) % NY) for y in range(NY)])


def norm_kernel(rows_ref, gain_ref, out_ref):
    rows = rows_ref[...].astype(F32)
    mean = jnp.mean(rows * rows, axis=-1, keepdims=True)
    out_ref[...] = (rows * lax.rsqrt(mean + 1e-06) * gain_ref[...]).astype(BF16)


def normed_rows(hidden, gain):
    rows, width = hidden.shape
    step = 64
    return pl.pallas_call(
        norm_kernel,
        grid=(rows // step,),
        in_specs=[
            pl.BlockSpec((step, width), lambda i: (i, 0)),
            pl.BlockSpec((width,), lambda i: (0,)),
        ],
        out_specs=pl.BlockSpec((step, width), lambda i: (i, 0)),
        out_shape=jax.ShapeDtypeStruct(hidden.shape, BF16),
        name="norm",
        cost_estimate=pl.CostEstimate(flops=2_000_000, bytes_accessed=2_400_000, transcendentals=128),
    )(hidden, gain)


def attended(scal, dy, q_ref, k_ref, v_ref, store):
    y, length = scal[3], scal[4]
    first = pl.multiple_of(lax.rem(y + dy, NY) * 128, 128)
    row = lax.broadcasted_iota(jnp.int32, (128, 512), 0) + first
    col = lax.broadcasted_iota(jnp.int32, (128, 512), 1)
    keep = (col <= row) & (col < length)
    for h in range(4):
        kv = slice((h // 2) * 128, (h // 2) * 128 + 128)
        score = lax.dot_general(
            q_ref[pl.ds(first, 128), h * 128 : h * 128 + 128],
            k_ref[:, kv],
            (((1,), (1,)), ((), ())),
            preferred_element_type=F32,
        )
        score = 50.0 * jnp.tanh(score * (1.0 / 50.0))
        score = jnp.where(keep, score, -1e30)
        top = jnp.max(score, axis=-1, keepdims=True)
        expo = jnp.exp(score - top)
        weights = (expo / jnp.sum(expo, axis=-1, keepdims=True)).astype(BF16)
        store(h, jnp.dot(weights, v_ref[:, kv], preferred_element_type=F32).astype(BF16))


def spread(att, wo, outs, width, chunk=1152):
    for at in range(0, width, chunk):
        partial = lax.dot_general(
            att[...], wo[at : at + chunk, :], (((1,), (1,)), ((), ())), preferred_element_type=F32
        )
        for ref, first in outs:
            ref[:, at : at + chunk] = partial[first : first + ref.shape[0]].astype(ref.dtype)


def copies(pairs, sem, then):
    for src, dst in pairs:
        copy = pltpu.make_async_copy(src, dst, sem)
        copy.start() if then == "start" else copy.wait()


def rows_of(xbuf, y, dy):
    return xbuf.at[pl.ds(pl.multiple_of(lax.rem(y + dy, NY) * 128, 128), 128)]


def shards_of(ref, table, wbuf, base):
    for j in range(ref.shape[0]):
        yield ref.at[j], wbuf.at[pl.ds(pl.multiple_of(table[base + j], 8), 72)]


def fill_kernel(offsets, groups, n_old, scal, table, *refs):
    c, y = scal[2], scal[3]
    xs, refs = refs[: len(offsets)], refs[len(offsets) :]
    ws, refs = refs[: len(groups)], refs[len(groups) :]
    either, (xbuf, wbuf, sem) = refs[:-3][: -n_old or None], refs[-3:]

    def run(then):
        copies([(ref, rows_of(xbuf, y, dy)) for ref, dy in zip(xs, offsets)], sem, then)
        for ref, group in zip(ws, groups):
            copies(shards_of(ref, table, wbuf, group * 4), sem, then)
        if either:
            for core, ref, base in ((0, either[0], 28), (1, either[1], 60)):

                @pl.when(c == core)
                def _():
                    copies(shards_of(ref, table, wbuf, base), sem, then)

    run("start")
    run("wait")


VMEM = pl.BlockSpec(memory_space=pltpu.VMEM)
SMEM = pl.BlockSpec(memory_space=pltpu.SMEM)


def fill(scal, table, xs, offsets, ws, groups, either, held, width):
    operands = [scal, table, *xs, *ws, *either, *held]
    n = len(operands)
    return pl.pallas_call(
        functools.partial(fill_kernel, offsets, groups, len(held)),
        in_specs=[SMEM] * 2 + [ANY] * (n - 2 - len(held)) + [VMEM] * len(held),
        out_specs=[VMEM] * 2,
        out_shape=[pltpu.VMEM((512, width), BF16), pltpu.VMEM((width, 1536), BF16)],
        scratch_shapes=[pltpu.SemaphoreType.DMA],
        input_output_aliases={n - 2: 0, n - 1: 1} if held else {},
        compiler_params=pltpu.CompilerParams(vmem_limit_bytes=SMALL_LIMIT),
        cost_estimate=pl.CostEstimate(flops=0, bytes_accessed=18_000_000, transcendentals=0),
    )(*operands)


def turned(raw, cos_ref, sin_ref, first, count):
    rows = pl.ds(first, count)
    return raw * cos_ref[rows, :] + pltpu.roll(raw, 64, 1) * sin_ref[rows, :]


def queries(scal, dy, xbuf, wbuf, cos_ref, sin_ref, q, slot):
    first = pl.multiple_of(lax.rem(scal[3] + dy, NY) * 128, 128)
    raw = jnp.dot(xbuf[pl.ds(first, 128), :], wbuf[:, 0:512], preferred_element_type=F32)
    for h in range(4):
        one = turned(raw[:, h * 128 : h * 128 + 128], cos_ref, sin_ref, first, 128)
        q[slot * 128 : slot * 128 + 128, h * 128 : h * 128 + 128] = (one * 144.0 ** (-0.5)).astype(BF16)


def attended(scal, dy, q, slot, k_ref, v_ref, att):
    y, length = scal[3], scal[4]
    first = lax.rem(y + dy, NY) * 128
    row = lax.broadcasted_iota(jnp.int32, (128, 512), 0) + first
    col = lax.broadcasted_iota(jnp.int32, (128, 512), 1)
    keep = (col <= row) & (col < length)
    mine = slice(slot * 128, slot * 128 + 128)
    for h in range(4):
        kv = slice((h // 2) * 128, (h // 2) * 128 + 128)
        head = slice(h * 128, h * 128 + 128)
        score = lax.dot_general(
            q[mine, head], k_ref[:, kv], (((1,), (1,)), ((), ())), preferred_element_type=F32
        )
        score = 50.0 * jnp.tanh(score * (1.0 / 50.0))
        score = jnp.where(keep, score, -1e30)
        top = jnp.max(score, axis=-1, keepdims=True)
        expo = jnp.exp(score - top)
        weights = (expo / jnp.sum(expo, axis=-1, keepdims=True)).astype(BF16)
        att[mine, head] = jnp.dot(weights, v_ref[:, kv], preferred_element_type=F32).astype(BF16)


def spread(att, wbuf, outs, chunk=1152):
    for at in range(0, wbuf.shape[0], chunk):
        partial = lax.dot_general(
            att[...], wbuf[at : at + chunk, 1024:1536], (((1,), (1,)), ((), ())), preferred_element_type=F32
        )
        for ref, first in outs:
            ref[:, at : at + chunk] = partial[first : first + ref.shape[0]].astype(ref.dtype)


def project_kernel(
    scal, table, cos_ref, sin_ref, w0, w1, up_own, down_own, up_other, down_other, xbuf, old,
    k_ref, v_ref, far0, far1, wbuf, q, att, sem,
):
    c, length = scal[2], scal[4]

    def run(then):
        for ref, group in ((w0, 13), (w1, 14)):
            copies(shards_of(ref, table, wbuf, group * 4), sem, then)
        for core, halves, base in ((0, (up_other, down_other), 60), (1, (up_own, down_own), 28)):

            @pl.when(c == core)
            def _():
                for i, ref in enumerate(halves):
                    copies(shards_of(ref, table, wbuf, base + 2 * i), sem, then)

    run("start")
    run("wait")
    live = lax.broadcasted_iota(jnp.int32, (512, 128), 0) < length
    raw = jnp.dot(xbuf[...], wbuf[:, 512:768], preferred_element_type=F32)
    for h in range(2):
        head = slice(h * 128, h * 128 + 128)
        k_ref[:, head] = jnp.where(live, turned(raw[:, head], cos_ref, sin_ref, 0, 512), 0.0).astype(BF16)
    raw = jnp.dot(xbuf[...], wbuf[:, 768:1024], preferred_element_type=F32)
    for h in range(2):
        head = slice(h * 128, h * 128 + 128)
        v_ref[:, head] = jnp.where(live, raw[:, head], 0.0).astype(BF16)
    queries(scal, 2, xbuf, wbuf, cos_ref, sin_ref, q, 0)
    attended(scal, 2, q, 0, k_ref, v_ref, att)
    spread(att, wbuf, ((far0, 0), (far1, 64)))


def project(scal, table, cosine, sine, arrays, xbuf, wbuf):
    width = wbuf.shape[0]
    outs = [(512, 256), (512, 256), (64, width), (64, width)]
    n = 4 + len(arrays)
    return pl.pallas_call(
        project_kernel,
        in_specs=[SMEM] * 2 + [VMEM] * 2 + [ANY] * len(arrays) + [VMEM] * 2,
        out_specs=[VMEM] * 5,
        out_shape=[jax.ShapeDtypeStruct(shape, BF16) for shape in outs] + [pltpu.VMEM(wbuf.shape, BF16)],
        scratch_shapes=[
            pltpu.VMEM((128, 512), BF16),
            pltpu.VMEM((128, 512), BF16),
            pltpu.SemaphoreType.DMA,
        ],
        input_output_aliases={n + 1: 4},
        compiler_params=pltpu.CompilerParams(vmem_limit_bytes=SMALL_LIMIT),
        name="project",
        cost_estimate=pl.CostEstimate(flops=4_000_000_000, bytes_accessed=10_000_000, transcendentals=524_288),
    )(scal, table, cosine, sine, *arrays, xbuf, wbuf)


def attend_kernel(blocks, outs, scal, cos_ref, sin_ref, k_ref, v_ref, xbuf, wbuf, *refs):
    out_refs, (q, att) = refs[:-2], refs[-2:]
    for slot, dy in enumerate(blocks):
        queries(scal, dy, xbuf, wbuf, cos_ref, sin_ref, q, slot)
        attended(scal, dy, q, slot, k_ref, v_ref, att)
    spread(att, wbuf, tuple(zip(out_refs, outs)))


def attend(scal, cosine, sine, key, value, xbuf, wbuf, blocks, outs, count):
    width = wbuf.shape[0]
    n = len(blocks)
    return pl.pallas_call(
        functools.partial(attend_kernel, blocks, outs),
        in_specs=[SMEM] + [VMEM] * 6,
        out_specs=[VMEM] * len(outs),
        out_shape=[jax.ShapeDtypeStruct((count, width), BF16)] * len(outs),
        scratch_shapes=[pltpu.VMEM((n * 128, 512), BF16)] * 2,
        compiler_params=pltpu.CompilerParams(vmem_limit_bytes=SMALL_LIMIT),
        cost_estimate=pl.CostEstimate(
            flops=n * 1_400_000_000, bytes_accessed=1_000_000 + n * 1_200_000, transcendentals=n * 524_288
        ),
    )(scal, cosine, sine, key, value, xbuf, wbuf)


def finish_kernel(scal, rows_ref, own_ref, a1, b0, gain_ref, a0_hbm, b1_hbm, out_hbm, a0, b1, out, sem, osem):
    y, length = scal[3], scal[4]
    first = pltpu.make_async_copy(a0_hbm, a0, sem.at[0])
    second = pltpu.make_async_copy(b1_hbm, b1, sem.at[1])
    first.start()
    second.start()
    gain = gain_ref[...]
    count = 32
    for i in range(4):
        if i % 2 == 0:
            (first, second)[i // 2].wait()
        rows = slice(i * count, i * count + count)
        here = slice(i % 2 * count, i % 2 * count + count)
        before, after = ((a0, b0), (a1, b1))[i // 2]
        total = own_ref[rows, :].astype(F32) + before[here, :].astype(F32) + after[here, :].astype(F32)
        mean = jnp.mean(total * total, axis=-1, keepdims=True)
        post = total * lax.rsqrt(mean + 1e-06) * gain
        row = lax.broadcasted_iota(jnp.int32, (count, 1), 0) + y * 128 + i * count
        out[rows, :] = jnp.where(row < length, rows_ref[rows, :].astype(F32) + post, 0.0).astype(BF16)
        pltpu.make_async_copy(out.at[rows], out_hbm.at[rows], osem).start()
    pltpu.make_async_copy(out, out_hbm, osem).wait()


def finish(scal, hidden, own, a0, a1, b0, b1, gain):
    width = hidden.shape[-1]
    return pl.pallas_call(
        finish_kernel,
        in_specs=[SMEM] + [VMEM] * 5 + [ANY] * 2,
        out_specs=ANY,
        out_shape=jax.ShapeDtypeStruct(hidden.shape, BF16),
        scratch_shapes=[
            pltpu.VMEM((64, width), BF16),
            pltpu.VMEM((64, width), BF16),
            pltpu.VMEM(hidden.shape, BF16),
            pltpu.SemaphoreType.DMA((2,)),
            pltpu.SemaphoreType.DMA,
        ],
        compiler_params=pltpu.CompilerParams(vmem_limit_bytes=SMALL_LIMIT),
        name="finish",
        cost_estimate=pl.CostEstimate(flops=6_000_000, bytes_accessed=7_000_000, transcendentals=128),
    )(scal, hidden, own, a1, b0, gain, a0, b1)


def angle_tables(maxlen):
    half = HD // 2
    freqs = 10000.0 ** (-jnp.arange(half, dtype=F32) / half)
    angles = jnp.arange(maxlen, dtype=jnp.int32).astype(F32)[:, None] * freqs[None, :]
    cosine, sine = jnp.cos(angles), jnp.sin(angles)
    return jnp.concatenate([cosine, cosine], -1), jnp.concatenate([-sine, sine], -1)


def torus(array, d, cores=(0, 1)):
    pairs = [
        (spot(z, x, c), spot(z + d[c][0], x + d[c][1], c))
        for z in range(NZ)
        for x in range(NX)
        for c in cores
    ]
    return lax.ppermute(array, "dp", pairs)


def one_way(array, source):
    pairs = [(spot(z, x, source), spot(z, x, 1 - source)) for z in range(NZ) for x in range(NX)]
    return lax.ppermute(array, "dp", pairs)


def swapped(array):
    return plane(array, dc=1)


SMALL_UP, SMALL_DOWN = ((1, 0), (0, 1)), ((-1, 0), (0, -1))
LARGE_UP, LARGE_DOWN = ((0, 1), (1, 0)), ((0, -1), (-1, 0))
NEAR, FAR = (0, -1, 1, -2), (2, -3, 3, 4)


def wrapped(dz, dx):
    return dz % NZ, dx % NX


PLACES_A = tuple(
    tuple(wrapped(dz, dx) for dz in zs)
    for zs, dx in ((NEAR, 0), (NEAR, -1), (NEAR, 1), (FAR, -1), (FAR, 1), (FAR, -2), (NEAR, 2), (FAR, 0))
)
PLACES_B = tuple(
    tuple(wrapped(dz, dx) for dx in NEAR) for dz in (0, -1, 1, -2, 2, -3, 3, -4)
)


def row_table(z, x, core):
    places = jnp.array([PLACES_A, PLACES_B], jnp.int32)
    rows = []
    for dc in range(2):
        owner = (core + dc) % 2
        mine = jnp.where(owner == 0, places[0], places[1])
        rows.append((((z + mine[..., 0]) % NZ * NX + (x + mine[..., 1]) % NX) * 2 + owner) * 72)
    return jnp.stack(rows).reshape(-1).astype(jnp.int32)


def gathered_weights(shard, core, tables):
    first = core == 0
    s1 = torus(shard, SMALL_UP)
    s2 = torus(shard, SMALL_DOWN)
    s3 = torus(s1, SMALL_UP)
    s4 = torus(s2, SMALL_DOWN)
    s5 = torus(s3, SMALL_UP)
    s6 = torus(s4, SMALL_DOWN)
    s7 = torus(s6, SMALL_DOWN)
    near = jnp.stack([shard, s1, s2, s3])
    r1 = torus(near, LARGE_UP)
    r2 = torus(near, LARGE_DOWN)
    r2, tables = lax.optimization_barrier((r2, tables))
    far = jnp.stack([s4, s5, s6, s7])
    r3 = torus(jnp.where(first, far, r1), LARGE_UP)
    r4 = torus(jnp.where(first, far, r2), LARGE_DOWN)
    r5 = torus(r3, LARGE_UP)
    r6 = torus(jnp.where(first, *lax.optimization_barrier((r2, r4))), LARGE_DOWN)
    r7 = torus(r5[:2], LARGE_UP, (1,))
    r8 = torus(r6[2:], LARGE_DOWN, (1,))
    arrays = [near, r1, r2, r3, r4, r5, r6]
    others = [swapped(a) for a in arrays]
    far = far, one_way(far, 0)
    up = r7, one_way(r7, 1)
    down = r8, one_way(r8, 1)
    return arrays, others, far, up, down, tables


def layer(hidden, lengths, norm_gain, w_query, w_key, w_value, w_out, post_gain):
    _, local_len, width = hidden.shape
    hidden = hidden.reshape(local_len, width)
    place = lax.axis_index("dp")
    core = place % 2
    scal = jnp.stack([place // 8, (place // 2) % 4, core, lax.axis_index("mp"), lengths[0]]).astype(jnp.int32)
    shard = jnp.concatenate([w_query, w_key, w_value, w_out.T], axis=1)
    normed = normed_rows(hidden, norm_gain)
    above, below = column(normed, -1), column(normed, 1)
    across = column(normed, 2)
    tables = (scal, row_table(scal[0], scal[1], core), *angle_tables(local_len * NY))
    arrays, others, far, up, down, tables = gathered_weights(shard, core, tables)
    scal, table, cosine, sine = tables
    held = fill(
        scal, table, [normed, above, below], (0, 1, 3), arrays[:3] + others[:3],
        (0, 1, 2, 8, 9, 10), far, (), width,
    )
    held = fill(scal, table, [across], (2,), arrays[3:5] + others[3:5], (3, 4, 11, 12), (), held, width)
    xbuf, wbuf = fill(scal, table, [], (), arrays[5:], (5, 6), (), held, width)
    rest = others[5:] + [up[0], down[0], up[1], down[1]]
    key, value, far0, far1, wbuf = project(scal, table, cosine, sine, rest, xbuf, wbuf)
    rfar0, rfar1 = column(far0, 1), column(far1, -1)
    up0, up1, down0, down1 = attend(scal, cosine, sine, key, value, xbuf, wbuf, (1, 3), (0, 64, 128, 192), 64)
    a1, b0 = column(up1, 1), column(down0, -1)
    (own,) = attend(scal, cosine, sine, key, value, xbuf, wbuf, (0,), (0,), 128)
    a0 = column((up0.astype(F32) + rfar0.astype(F32)).astype(BF16), 1)
    b1 = column((down1.astype(F32) + rfar1.astype(F32)).astype(BF16), -1)
    mixed = finish(scal, hidden, own, a0, a1, b0, b1, post_gain)
    return mixed[None], key[None], value[None]


def solution(mesh):
    return jax.shard_map(
        layer,
        mesh=mesh,
        in_specs=(
            P("dp", "mp", None),
            P("dp"),
            P(),
            P("dp", "mp"),
            P("dp", "mp"),
            P("dp", "mp"),
            P("mp", "dp"),
            P(),
        ),
        out_specs=(P("dp", "mp", None), P("dp", None, "mp"), P("dp", None, "mp")),
        check_vma=False,
    )
```

```python
import functools

import jax
import jax.numpy as jnp
from jax import lax
from jax.experimental import pallas as pl
from jax.experimental.pallas import tpu as pltpu
from jax.sharding import PartitionSpec as P


HD = 128
NZ, NX, NY = 8, 4, 4
F32 = jnp.float32
BF16 = jnp.bfloat16
ANY = pl.BlockSpec(memory_space=pl.ANY)
SMALL_LIMIT = 24 * 1024 * 1024


def spot(z, x, c):
    return ((z % NZ) * NX + (x % NX)) * 2 + c


def plane(array, dz=0, dx=0, dc=0):
    pairs = [
        (spot(z, x, c), spot(z + dz, x + dx, c ^ dc))
        for z in range(NZ)
        for x in range(NX)
        for c in range(2)
    ]
    return lax.ppermute(array, "dp", pairs)


def column(array, dy):
    return lax.ppermute(array, "mp", [(y, (y + dy) % NY) for y in range(NY)])


def norm_kernel(rows_ref, gain_ref, out_ref):
    rows = rows_ref[...].astype(F32)
    mean = jnp.mean(rows * rows, axis=-1, keepdims=True)
    out_ref[...] = (rows * lax.rsqrt(mean + 1e-06) * gain_ref[...]).astype(BF16)


def normed_rows(hidden, gain):
    rows, width = hidden.shape
    step = 64
    return pl.pallas_call(
        norm_kernel,
        grid=(rows // step,),
        in_specs=[
            pl.BlockSpec((step, width), lambda i: (i, 0)),
            pl.BlockSpec((width,), lambda i: (0,)),
        ],
        out_specs=pl.BlockSpec((step, width), lambda i: (i, 0)),
        out_shape=jax.ShapeDtypeStruct(hidden.shape, BF16),
        name="norm",
        cost_estimate=pl.CostEstimate(flops=2_000_000, bytes_accessed=2_400_000, transcendentals=128),
    )(hidden, gain)


def attended(scal, dy, q_ref, k_ref, v_ref, store):
    y, length = scal[3], scal[4]
    first = pl.multiple_of(lax.rem(y + dy, NY) * 128, 128)
    row = lax.broadcasted_iota(jnp.int32, (128, 512), 0) + first
    col = lax.broadcasted_iota(jnp.int32, (128, 512), 1)
    keep = (col <= row) & (col < length)
    for h in range(4):
        kv = slice((h // 2) * 128, (h // 2) * 128 + 128)
        score = lax.dot_general(
            q_ref[pl.ds(first, 128), h * 128 : h * 128 + 128],
            k_ref[:, kv],
            (((1,), (1,)), ((), ())),
            preferred_element_type=F32,
        )
        score = 50.0 * jnp.tanh(score * (1.0 / 50.0))
        score = jnp.where(keep, score, -1e30)
        top = jnp.max(score, axis=-1, keepdims=True)
        expo = jnp.exp(score - top)
        weights = (expo / jnp.sum(expo, axis=-1, keepdims=True)).astype(BF16)
        store(h, jnp.dot(weights, v_ref[:, kv], preferred_element_type=F32).astype(BF16))


def spread(att, wo, outs, width, chunk=1152):
    for at in range(0, width, chunk):
        partial = lax.dot_general(
            att[...], wo[at : at + chunk, :], (((1,), (1,)), ((), ())), preferred_element_type=F32
        )
        for ref, first in outs:
            ref[:, at : at + chunk] = partial[first : first + ref.shape[0]].astype(ref.dtype)


def copies(pairs, sem, then):
    for src, dst in pairs:
        copy = pltpu.make_async_copy(src, dst, sem)
        copy.start() if then == "start" else copy.wait()


def rows_of(xbuf, y, dy, first, count):
    return xbuf.at[pl.ds(pl.multiple_of(lax.rem(y + dy, NY) * 128 + first, 64), count)]


def shards_of(ref, table, wbuf, base):
    for j in range(ref.shape[0]):
        yield ref.at[j], wbuf.at[pl.ds(pl.multiple_of(table[base + j], 8), 72)]


def fill_kernel(offsets, groups, n_old, scal, table, *refs):
    c, y = scal[2], scal[3]
    xs, refs = refs[: len(offsets)], refs[len(offsets) :]
    ws, refs = refs[: len(groups)], refs[len(groups) :]
    either, (xbuf, wbuf, sem) = refs[:-3][: -n_old or None], refs[-3:]

    def run(then):
        copies([(ref, rows_of(xbuf, y, *at, ref.shape[0])) for ref, at in zip(xs, offsets)], sem, then)
        for ref, group in zip(ws, groups):
            copies(shards_of(ref, table, wbuf, group * 4), sem, then)
        if either:
            for core, ref, base in ((0, either[0], 28), (1, either[1], 60)):

                @pl.when(c == core)
                def _():
                    copies(shards_of(ref, table, wbuf, base), sem, then)

    run("start")
    run("wait")


VMEM = pl.BlockSpec(memory_space=pltpu.VMEM)
SMEM = pl.BlockSpec(memory_space=pltpu.SMEM)


def fill(scal, table, xs, offsets, ws, groups, either, held, width):
    operands = [scal, table, *xs, *ws, *either, *held]
    n = len(operands)
    return pl.pallas_call(
        functools.partial(fill_kernel, offsets, groups, len(held)),
        in_specs=[SMEM] * 2 + [ANY] * (n - 2 - len(held)) + [VMEM] * len(held),
        out_specs=[VMEM] * 2,
        out_shape=[pltpu.VMEM((512, width), BF16), pltpu.VMEM((width, 1536), BF16)],
        scratch_shapes=[pltpu.SemaphoreType.DMA],
        input_output_aliases={n - 2: 0, n - 1: 1} if held else {},
        compiler_params=pltpu.CompilerParams(vmem_limit_bytes=SMALL_LIMIT),
        cost_estimate=pl.CostEstimate(flops=0, bytes_accessed=18_000_000, transcendentals=0),
    )(*operands)


def turned(raw, cos_ref, sin_ref, first, count):
    rows = pl.ds(first, count)
    return raw * cos_ref[rows, :] + pltpu.roll(raw, 64, 1) * sin_ref[rows, :]


def queries(scal, dy, xbuf, wbuf, cos_ref, sin_ref, q, slot):
    first = pl.multiple_of(lax.rem(scal[3] + dy, NY) * 128, 128)
    raw = jnp.dot(xbuf[pl.ds(first, 128), :], wbuf[:, 0:512], preferred_element_type=F32)
    for h in range(4):
        one = turned(raw[:, h * 128 : h * 128 + 128], cos_ref, sin_ref, first, 128)
        q[slot * 128 : slot * 128 + 128, h * 128 : h * 128 + 128] = (one * 144.0 ** (-0.5)).astype(BF16)


def attended(scal, dy, q, slot, k_ref, v_ref, att):
    y, length = scal[3], scal[4]
    first = lax.rem(y + dy, NY) * 128
    row = lax.broadcasted_iota(jnp.int32, (128, 512), 0) + first
    col = lax.broadcasted_iota(jnp.int32, (128, 512), 1)
    keep = (col <= row) & (col < length)
    mine = slice(slot * 128, slot * 128 + 128)
    for h in range(4):
        kv = slice((h // 2) * 128, (h // 2) * 128 + 128)
        head = slice(h * 128, h * 128 + 128)
        score = lax.dot_general(
            q[mine, head], k_ref[:, kv], (((1,), (1,)), ((), ())), preferred_element_type=F32
        )
        score = 50.0 * jnp.tanh(score * (1.0 / 50.0))
        score = jnp.where(keep, score, -1e30)
        top = jnp.max(score, axis=-1, keepdims=True)
        expo = jnp.exp(score - top)
        weights = (expo / jnp.sum(expo, axis=-1, keepdims=True)).astype(BF16)
        att[mine, head] = jnp.dot(weights, v_ref[:, kv], preferred_element_type=F32).astype(BF16)


def spread(att, wbuf, outs, chunk=1152):
    for at in range(0, wbuf.shape[0], chunk):
        partial = lax.dot_general(
            att[...], wbuf[at : at + chunk, 1024:1536], (((1,), (1,)), ((), ())), preferred_element_type=F32
        )
        for ref, first in outs:
            ref[:, at : at + chunk] = partial[first : first + ref.shape[0]].astype(ref.dtype)


def project_kernel(
    scal, table, cos_ref, sin_ref, up_own, down_own, up_other, down_other, xbuf, old,
    k_ref, v_ref, far0, far1, wbuf, q, att, sem,
):
    c, length = scal[2], scal[4]

    def run(then):
        for core, halves, base in ((0, (up_other, down_other), 60), (1, (up_own, down_own), 28)):

            @pl.when(c == core)
            def _():
                for i, ref in enumerate(halves):
                    copies(shards_of(ref, table, wbuf, base + 2 * i), sem, then)

    run("start")
    run("wait")
    live = lax.broadcasted_iota(jnp.int32, (512, 128), 0) < length
    raw = jnp.dot(xbuf[...], wbuf[:, 512:768], preferred_element_type=F32)
    for h in range(2):
        head = slice(h * 128, h * 128 + 128)
        k_ref[:, head] = jnp.where(live, turned(raw[:, head], cos_ref, sin_ref, 0, 512), 0.0).astype(BF16)
    raw = jnp.dot(xbuf[...], wbuf[:, 768:1024], preferred_element_type=F32)
    for h in range(2):
        head = slice(h * 128, h * 128 + 128)
        v_ref[:, head] = jnp.where(live, raw[:, head], 0.0).astype(BF16)
    queries(scal, 2, xbuf, wbuf, cos_ref, sin_ref, q, 0)
    attended(scal, 2, q, 0, k_ref, v_ref, att)
    spread(att, wbuf, ((far0, 0), (far1, 64)))


def project(scal, table, cosine, sine, arrays, xbuf, wbuf):
    width = wbuf.shape[0]
    outs = [(512, 256), (512, 256), (64, width), (64, width)]
    n = 4 + len(arrays)
    return pl.pallas_call(
        project_kernel,
        in_specs=[SMEM] * 2 + [VMEM] * 2 + [ANY] * len(arrays) + [VMEM] * 2,
        out_specs=[VMEM] * 5,
        out_shape=[jax.ShapeDtypeStruct(shape, BF16) for shape in outs] + [pltpu.VMEM(wbuf.shape, BF16)],
        scratch_shapes=[
            pltpu.VMEM((128, 512), BF16),
            pltpu.VMEM((128, 512), BF16),
            pltpu.SemaphoreType.DMA,
        ],
        input_output_aliases={n + 1: 4},
        compiler_params=pltpu.CompilerParams(vmem_limit_bytes=SMALL_LIMIT),
        name="project",
        cost_estimate=pl.CostEstimate(flops=4_000_000_000, bytes_accessed=10_000_000, transcendentals=524_288),
    )(scal, table, cosine, sine, *arrays, xbuf, wbuf)


def attend_kernel(blocks, outs, scal, cos_ref, sin_ref, k_ref, v_ref, xbuf, wbuf, *refs):
    out_refs, (q, att) = refs[:-2], refs[-2:]
    for slot, dy in enumerate(blocks):
        queries(scal, dy, xbuf, wbuf, cos_ref, sin_ref, q, slot)
        attended(scal, dy, q, slot, k_ref, v_ref, att)
    spread(att, wbuf, tuple(zip(out_refs, outs)))


def attend(scal, cosine, sine, key, value, xbuf, wbuf, blocks, outs, count):
    width = wbuf.shape[0]
    n = len(blocks)
    return pl.pallas_call(
        functools.partial(attend_kernel, blocks, outs),
        in_specs=[SMEM] + [VMEM] * 6,
        out_specs=[VMEM] * len(outs),
        out_shape=[jax.ShapeDtypeStruct((count, width), BF16)] * len(outs),
        scratch_shapes=[pltpu.VMEM((n * 128, 512), BF16)] * 2,
        compiler_params=pltpu.CompilerParams(vmem_limit_bytes=SMALL_LIMIT),
        cost_estimate=pl.CostEstimate(
            flops=n * 1_400_000_000, bytes_accessed=1_000_000 + n * 1_200_000, transcendentals=n * 524_288
        ),
    )(scal, cosine, sine, key, value, xbuf, wbuf)


def finish_kernel(scal, rows_ref, own_ref, a1, b0, gain_ref, a0_hbm, b1_hbm, out_hbm, a0, b1, out, sem, osem):
    y, length = scal[3], scal[4]
    first = pltpu.make_async_copy(a0_hbm, a0, sem.at[0])
    second = pltpu.make_async_copy(b1_hbm, b1, sem.at[1])
    first.start()
    second.start()
    gain = gain_ref[...]
    count = 32
    for i in range(4):
        if i % 2 == 0:
            (first, second)[i // 2].wait()
        rows = slice(i * count, i * count + count)
        here = slice(i % 2 * count, i % 2 * count + count)
        before, after = ((a0, b0), (a1, b1))[i // 2]
        total = own_ref[rows, :].astype(F32) + before[here, :].astype(F32) + after[here, :].astype(F32)
        mean = jnp.mean(total * total, axis=-1, keepdims=True)
        post = total * lax.rsqrt(mean + 1e-06) * gain
        row = lax.broadcasted_iota(jnp.int32, (count, 1), 0) + y * 128 + i * count
        out[rows, :] = jnp.where(row < length, rows_ref[rows, :].astype(F32) + post, 0.0).astype(BF16)
        pltpu.make_async_copy(out.at[rows], out_hbm.at[rows], osem).start()
    pltpu.make_async_copy(out, out_hbm, osem).wait()


def finish(scal, hidden, own, a0, a1, b0, b1, gain):
    width = hidden.shape[-1]
    return pl.pallas_call(
        finish_kernel,
        in_specs=[SMEM] + [VMEM] * 5 + [ANY] * 2,
        out_specs=ANY,
        out_shape=jax.ShapeDtypeStruct(hidden.shape, BF16),
        scratch_shapes=[
            pltpu.VMEM((64, width), BF16),
            pltpu.VMEM((64, width), BF16),
            pltpu.VMEM(hidden.shape, BF16),
            pltpu.SemaphoreType.DMA((2,)),
            pltpu.SemaphoreType.DMA,
        ],
        compiler_params=pltpu.CompilerParams(vmem_limit_bytes=SMALL_LIMIT),
        name="finish",
        cost_estimate=pl.CostEstimate(flops=6_000_000, bytes_accessed=7_000_000, transcendentals=128),
    )(scal, hidden, own, a1, b0, gain, a0, b1)


def angle_tables(maxlen):
    half = HD // 2
    freqs = 10000.0 ** (-jnp.arange(half, dtype=F32) / half)
    angles = jnp.arange(maxlen, dtype=jnp.int32).astype(F32)[:, None] * freqs[None, :]
    cosine, sine = jnp.cos(angles), jnp.sin(angles)
    return jnp.concatenate([cosine, cosine], -1), jnp.concatenate([-sine, sine], -1)


def torus(array, d, cores=(0, 1)):
    pairs = [
        (spot(z, x, c), spot(z + d[c][0], x + d[c][1], c))
        for z in range(NZ)
        for x in range(NX)
        for c in cores
    ]
    return lax.ppermute(array, "dp", pairs)


def one_way(array, source):
    pairs = [(spot(z, x, source), spot(z, x, 1 - source)) for z in range(NZ) for x in range(NX)]
    return lax.ppermute(array, "dp", pairs)


def swapped(array):
    return plane(array, dc=1)


SMALL_UP, SMALL_DOWN = ((1, 0), (0, 1)), ((-1, 0), (0, -1))
LARGE_UP, LARGE_DOWN = ((0, 1), (1, 0)), ((0, -1), (-1, 0))
NEAR, FAR = (0, -1, 1, -2), (2, -3, 3, 4)


def wrapped(dz, dx):
    return dz % NZ, dx % NX


PLACES_A = tuple(
    tuple(wrapped(dz, dx) for dz in zs)
    for zs, dx in ((NEAR, 0), (NEAR, -1), (NEAR, 1), (FAR, -1), (FAR, 1), (FAR, -2), (NEAR, 2), (FAR, 0))
)
PLACES_B = tuple(
    tuple(wrapped(dz, dx) for dx in NEAR) for dz in (0, -1, 1, -2, 2, -3, 3, -4)
)


def row_table(z, x, core):
    places = jnp.array([PLACES_A, PLACES_B], jnp.int32)
    rows = []
    for dc in range(2):
        owner = (core + dc) % 2
        mine = jnp.where(owner == 0, places[0], places[1])
        rows.append((((z + mine[..., 0]) % NZ * NX + (x + mine[..., 1]) % NX) * 2 + owner) * 72)
    return jnp.stack(rows).reshape(-1).astype(jnp.int32)


def gathered_weights(shard, core, tables):
    first = core == 0
    s1 = torus(shard, SMALL_UP)
    s2 = torus(shard, SMALL_DOWN)
    s3 = torus(s1, SMALL_UP)
    s4 = torus(s2, SMALL_DOWN)
    s5 = torus(s3, SMALL_UP)
    s6 = torus(s4, SMALL_DOWN)
    s7 = torus(s6, SMALL_DOWN)
    near = jnp.stack([shard, s1, s2, s3])
    r1 = torus(near, LARGE_UP)
    r2 = torus(near, LARGE_DOWN)
    r2, tables = lax.optimization_barrier((r2, tables))
    far = jnp.stack([s4, s5, s6, s7])
    r3 = torus(jnp.where(first, far, r1), LARGE_UP)
    r4 = torus(jnp.where(first, far, r2), LARGE_DOWN)
    r5 = torus(r3, LARGE_UP)
    r6 = torus(jnp.where(first, *lax.optimization_barrier((r2, r4))), LARGE_DOWN)
    r7 = torus(r5[:2], LARGE_UP, (1,))
    r8 = torus(r6[2:], LARGE_DOWN, (1,))
    arrays = [near, r1, r2, r3, r4, r5, r6]
    others = [swapped(a) for a in arrays]
    far = far, one_way(far, 0)
    up = r7, one_way(r7, 1)
    down = r8, one_way(r8, 1)
    return arrays, others, far, up, down, tables


def layer(hidden, lengths, norm_gain, w_query, w_key, w_value, w_out, post_gain):
    _, local_len, width = hidden.shape
    hidden = hidden.reshape(local_len, width)
    place = lax.axis_index("dp")
    core = place % 2
    scal = jnp.stack([place // 8, (place // 2) % 4, core, lax.axis_index("mp"), lengths[0]]).astype(jnp.int32)
    shard = jnp.concatenate([w_query, w_key, w_value, w_out.T], axis=1)
    normed = normed_rows(hidden, norm_gain)
    above, below = column(normed, -1), column(normed, 1)
    across0 = column(above[:64], -1)
    across1 = column(below[64:], 1)
    tables = (scal, row_table(scal[0], scal[1], core), *angle_tables(local_len * NY))
    arrays, others, far, up, down, tables = gathered_weights(shard, core, tables)
    scal, table, cosine, sine = tables
    held = fill(
        scal, table, [normed, above, below], ((0, 0), (1, 0), (3, 0)), arrays[:3] + others[:3],
        (0, 1, 2, 8, 9, 10), far, (), width,
    )
    held = fill(
        scal, table, [across0, across1], ((2, 0), (2, 64)), arrays[3:5] + others[3:5], (3, 4, 11, 12), (), held, width
    )
    xbuf, wbuf = fill(scal, table, [], (), arrays[5:] + others[5:], (5, 6, 13, 14), (), held, width)
    rest = [up[0], down[0], up[1], down[1]]
    key, value, far0, far1, wbuf = project(scal, table, cosine, sine, rest, xbuf, wbuf)
    rfar0, rfar1 = column(far0, 1), column(far1, -1)
    up0, up1, down0, down1 = attend(scal, cosine, sine, key, value, xbuf, wbuf, (1, 3), (0, 64, 128, 192), 64)
    a1, b0 = column(up1, 1), column(down0, -1)
    (own,) = attend(scal, cosine, sine, key, value, xbuf, wbuf, (0,), (0,), 128)
    a0 = column((up0.astype(F32) + rfar0.astype(F32)).astype(BF16), 1)
    b1 = column((down1.astype(F32) + rfar1.astype(F32)).astype(BF16), -1)
    mixed = finish(scal, hidden, own, a0, a1, b0, b1, post_gain)
    return mixed[None], key[None], value[None]


def solution(mesh):
    return jax.shard_map(
        layer,
        mesh=mesh,
        in_specs=(
            P("dp", "mp", None),
            P("dp"),
            P(),
            P("dp", "mp"),
            P("dp", "mp"),
            P("dp", "mp"),
            P("mp", "dp"),
            P(),
        ),
        out_specs=(P("dp", "mp", None), P("dp", None, "mp"), P("dp", None, "mp")),
        check_vma=False,
    )
```

```python
import functools

import jax
import jax.numpy as jnp
from jax import lax
from jax.experimental import pallas as pl
from jax.experimental.pallas import tpu as pltpu
from jax.sharding import PartitionSpec as P


HD = 128
NZ, NX, NY = 8, 4, 4
F32 = jnp.float32
BF16 = jnp.bfloat16
ANY = pl.BlockSpec(memory_space=pl.ANY)
SMALL_LIMIT = 24 * 1024 * 1024


def spot(z, x, c):
    return ((z % NZ) * NX + (x % NX)) * 2 + c


def plane(array, dz=0, dx=0, dc=0):
    pairs = [
        (spot(z, x, c), spot(z + dz, x + dx, c ^ dc))
        for z in range(NZ)
        for x in range(NX)
        for c in range(2)
    ]
    return lax.ppermute(array, "dp", pairs)


def column(array, dy):
    return lax.ppermute(array, "mp", [(y, (y + dy) % NY) for y in range(NY)])


def norm_kernel(rows_ref, gain_ref, out_ref):
    rows = rows_ref[...].astype(F32)
    mean = jnp.mean(rows * rows, axis=-1, keepdims=True)
    out_ref[...] = (rows * lax.rsqrt(mean + 1e-06) * gain_ref[...]).astype(BF16)


def normed_rows(hidden, gain):
    rows, width = hidden.shape
    step = 64
    return pl.pallas_call(
        norm_kernel,
        grid=(rows // step,),
        in_specs=[
            pl.BlockSpec((step, width), lambda i: (i, 0)),
            pl.BlockSpec((width,), lambda i: (0,)),
        ],
        out_specs=pl.BlockSpec((step, width), lambda i: (i, 0)),
        out_shape=jax.ShapeDtypeStruct(hidden.shape, BF16),
        name="norm",
        cost_estimate=pl.CostEstimate(flops=2_000_000, bytes_accessed=2_400_000, transcendentals=128),
    )(hidden, gain)


def attended(scal, dy, q_ref, k_ref, v_ref, store):
    y, length = scal[3], scal[4]
    first = pl.multiple_of(lax.rem(y + dy, NY) * 128, 128)
    row = lax.broadcasted_iota(jnp.int32, (128, 512), 0) + first
    col = lax.broadcasted_iota(jnp.int32, (128, 512), 1)
    keep = (col <= row) & (col < length)
    for h in range(4):
        kv = slice((h // 2) * 128, (h // 2) * 128 + 128)
        score = lax.dot_general(
            q_ref[pl.ds(first, 128), h * 128 : h * 128 + 128],
            k_ref[:, kv],
            (((1,), (1,)), ((), ())),
            preferred_element_type=F32,
        )
        score = 50.0 * jnp.tanh(score * (1.0 / 50.0))
        score = jnp.where(keep, score, -1e30)
        top = jnp.max(score, axis=-1, keepdims=True)
        expo = jnp.exp(score - top)
        weights = (expo / jnp.sum(expo, axis=-1, keepdims=True)).astype(BF16)
        store(h, jnp.dot(weights, v_ref[:, kv], preferred_element_type=F32).astype(BF16))


def spread(att, wo, outs, width, chunk=1152):
    for at in range(0, width, chunk):
        partial = lax.dot_general(
            att[...], wo[at : at + chunk, :], (((1,), (1,)), ((), ())), preferred_element_type=F32
        )
        for ref, first in outs:
            ref[:, at : at + chunk] = partial[first : first + ref.shape[0]].astype(ref.dtype)


def start(pairs, sem):
    for src, dst in pairs:
        pltpu.make_async_copy(src, dst, sem).start()


def finished(target, rows, sem):
    part = target.at[pl.ds(0, rows)]
    pltpu.make_async_copy(part, part, sem).wait()


def rows_of(xbuf, y, dy, first, count):
    return xbuf.at[pl.ds(pl.multiple_of(lax.rem(y + dy, NY) * 128 + first, 64), count)]


def shards_of(ref, table, wbuf, base):
    for j in range(ref.shape[0]):
        yield ref.at[j], wbuf.at[pl.ds(pl.multiple_of(table[base + j], 8), 72)]


def fill_kernel(offsets, groups, n_old, scal, table, *refs):
    c, y = scal[2], scal[3]
    xs, refs = refs[: len(offsets)], refs[len(offsets) :]
    ws, refs = refs[: len(groups)], refs[len(groups) :]
    either, (xbuf, wbuf, sem) = refs[:-3][: -n_old or None], refs[-3:]

    for ref, at in zip(xs, offsets):
        pltpu.make_async_copy(ref, rows_of(xbuf, y, *at, ref.shape[0]), sem.at[0]).start()
    for ref, group in zip(ws, groups):
        start(shards_of(ref, table, wbuf, group * 4), sem.at[1])
    if either:
        for core, ref, base in ((0, either[0], 28), (1, either[1], 60)):

            @pl.when(c == core)
            def _():
                start(shards_of(ref, table, wbuf, base), sem.at[1])

    if xs:
        finished(xbuf, sum(ref.shape[0] for ref in xs), sem.at[0])
    finished(wbuf, 72 * 4 * (len(groups) + bool(either)), sem.at[1])


VMEM = pl.BlockSpec(memory_space=pltpu.VMEM)
SMEM = pl.BlockSpec(memory_space=pltpu.SMEM)


def fill(scal, table, xs, offsets, ws, groups, either, held, width):
    operands = [scal, table, *xs, *ws, *either, *held]
    n = len(operands)
    return pl.pallas_call(
        functools.partial(fill_kernel, offsets, groups, len(held)),
        in_specs=[SMEM] * 2 + [ANY] * (n - 2 - len(held)) + [VMEM] * len(held),
        out_specs=[VMEM] * 2,
        out_shape=[pltpu.VMEM((512, width), BF16), pltpu.VMEM((width, 1536), BF16)],
        scratch_shapes=[pltpu.SemaphoreType.DMA((2,))],
        input_output_aliases={n - 2: 0, n - 1: 1} if held else {},
        compiler_params=pltpu.CompilerParams(vmem_limit_bytes=SMALL_LIMIT),
        cost_estimate=pl.CostEstimate(flops=0, bytes_accessed=18_000_000, transcendentals=0),
    )(*operands)


def turned(raw, cos_ref, sin_ref, first, count):
    rows = pl.ds(first, count)
    return raw * cos_ref[rows, :] + pltpu.roll(raw, 64, 1) * sin_ref[rows, :]


def queries(scal, dy, xbuf, wbuf, cos_ref, sin_ref, q, slot):
    first = pl.multiple_of(lax.rem(scal[3] + dy, NY) * 128, 128)
    raw = jnp.dot(xbuf[pl.ds(first, 128), :], wbuf[:, 0:512], preferred_element_type=F32)
    for h in range(4):
        one = turned(raw[:, h * 128 : h * 128 + 128], cos_ref, sin_ref, first, 128)
        q[pl.ds(slot * 128, 128), h * 128 : h * 128 + 128] = (one * 144.0 ** (-0.5)).astype(BF16)


def attended(scal, dy, q, slot, k_ref, v_ref, att):
    y, length = scal[3], scal[4]
    first = lax.rem(y + dy, NY) * 128
    row = lax.broadcasted_iota(jnp.int32, (128, 512), 0) + first
    col = lax.broadcasted_iota(jnp.int32, (128, 512), 1)
    keep = (col <= row) & (col < length)
    mine = pl.ds(slot * 128, 128)
    for h in range(4):
        kv = slice((h // 2) * 128, (h // 2) * 128 + 128)
        head = slice(h * 128, h * 128 + 128)
        score = lax.dot_general(
            q[mine, head], k_ref[:, kv], (((1,), (1,)), ((), ())), preferred_element_type=F32
        )
        score = 50.0 * jnp.tanh(score * (1.0 / 50.0))
        score = jnp.where(keep, score, -1e30)
        top = jnp.max(score, axis=-1, keepdims=True)
        expo = jnp.exp(score - top)
        weights = (expo / jnp.sum(expo, axis=-1, keepdims=True)).astype(BF16)
        att[mine, head] = jnp.dot(weights, v_ref[:, kv], preferred_element_type=F32).astype(BF16)


def spread(att, wbuf, outs, chunk=1152):
    for at in range(0, wbuf.shape[0], chunk):
        partial = lax.dot_general(
            att[...], wbuf[at : at + chunk, 1024:1536], (((1,), (1,)), ((), ())), preferred_element_type=F32
        )
        for ref, first in outs:
            ref[:, at : at + chunk] = partial[first : first + ref.shape[0]].astype(ref.dtype)


def project_kernel(
    scal, table, cos_ref, sin_ref, up_own, down_own, up_other, down_other, xbuf, old,
    k_ref, v_ref, far0, far1, wbuf, q, att, sem,
):
    c, length = scal[2], scal[4]

    for core, halves, base in ((0, (up_other, down_other), 60), (1, (up_own, down_own), 28)):

        @pl.when(c == core)
        def _():
            for i, ref in enumerate(halves):
                start(shards_of(ref, table, wbuf, base + 2 * i), sem)

    finished(wbuf, 72 * 4, sem)
    live = lax.broadcasted_iota(jnp.int32, (512, 128), 0) < length
    raw = jnp.dot(xbuf[...], wbuf[:, 512:768], preferred_element_type=F32)
    for h in range(2):
        head = slice(h * 128, h * 128 + 128)
        k_ref[:, head] = jnp.where(live, turned(raw[:, head], cos_ref, sin_ref, 0, 512), 0.0).astype(BF16)
    raw = jnp.dot(xbuf[...], wbuf[:, 768:1024], preferred_element_type=F32)
    for h in range(2):
        head = slice(h * 128, h * 128 + 128)
        v_ref[:, head] = jnp.where(live, raw[:, head], 0.0).astype(BF16)
    queries(scal, 2, xbuf, wbuf, cos_ref, sin_ref, q, 0)
    attended(scal, 2, q, 0, k_ref, v_ref, att)
    spread(att, wbuf, ((far0, 0), (far1, 64)))


def project(scal, table, cosine, sine, arrays, xbuf, wbuf):
    width = wbuf.shape[0]
    outs = [(512, 256), (512, 256), (64, width), (64, width)]
    n = 4 + len(arrays)
    return pl.pallas_call(
        project_kernel,
        in_specs=[SMEM] * 2 + [VMEM] * 2 + [ANY] * len(arrays) + [VMEM] * 2,
        out_specs=[VMEM] * 5,
        out_shape=[jax.ShapeDtypeStruct(shape, BF16) for shape in outs] + [pltpu.VMEM(wbuf.shape, BF16)],
        scratch_shapes=[
            pltpu.VMEM((128, 512), BF16),
            pltpu.VMEM((128, 512), BF16),
            pltpu.SemaphoreType.DMA,
        ],
        input_output_aliases={n + 1: 4},
        compiler_params=pltpu.CompilerParams(vmem_limit_bytes=SMALL_LIMIT),
        name="project",
        cost_estimate=pl.CostEstimate(flops=4_000_000_000, bytes_accessed=10_000_000, transcendentals=524_288),
    )(scal, table, cosine, sine, *arrays, xbuf, wbuf)


def attend_kernel(blocks, outs, scal, cos_ref, sin_ref, k_ref, v_ref, xbuf, wbuf, *refs):
    out_refs, (q, att) = refs[:-2], refs[-2:]
    stride = blocks[-1] - blocks[0]

    def block(slot, carry):
        dy = blocks[0] + slot * stride
        queries(scal, dy, xbuf, wbuf, cos_ref, sin_ref, q, slot)
        attended(scal, dy, q, slot, k_ref, v_ref, att)
        return carry

    lax.fori_loop(0, len(blocks), block, 0)
    chunk = 1152

    def stretch(i, carry):
        at = pl.multiple_of(i * chunk, 128)
        partial = lax.dot_general(
            att[...], wbuf[pl.ds(at, chunk), 1024:1536], (((1,), (1,)), ((), ())), preferred_element_type=F32
        )
        for ref, first in zip(out_refs, outs):
            ref[:, pl.ds(at, chunk)] = partial[first : first + ref.shape[0]].astype(ref.dtype)
        return carry

    lax.fori_loop(0, wbuf.shape[0] // chunk, stretch, 0)


def attend(scal, cosine, sine, key, value, xbuf, wbuf, blocks, outs, count):
    width = wbuf.shape[0]
    n = len(blocks)
    return pl.pallas_call(
        functools.partial(attend_kernel, blocks, outs),
        in_specs=[SMEM] + [VMEM] * 6,
        out_specs=[VMEM] * len(outs),
        out_shape=[jax.ShapeDtypeStruct((count, width), BF16)] * len(outs),
        scratch_shapes=[pltpu.VMEM((n * 128, 512), BF16)] * 2,
        compiler_params=pltpu.CompilerParams(vmem_limit_bytes=SMALL_LIMIT),
        cost_estimate=pl.CostEstimate(
            flops=n * 1_400_000_000, bytes_accessed=1_000_000 + n * 1_200_000, transcendentals=n * 524_288
        ),
    )(scal, cosine, sine, key, value, xbuf, wbuf)


def finish_kernel(scal, rows_ref, own_ref, a1, b0, gain_ref, a0_hbm, b1_hbm, out_hbm, a0, b1, out, sem, osem):
    y, length = scal[3], scal[4]
    first = pltpu.make_async_copy(a0_hbm, a0, sem.at[0])
    second = pltpu.make_async_copy(b1_hbm, b1, sem.at[1])
    first.start()
    second.start()
    gain = gain_ref[...]
    count = 32
    for i in range(4):
        if i % 2 == 0:
            (first, second)[i // 2].wait()
        rows = slice(i * count, i * count + count)
        here = slice(i % 2 * count, i % 2 * count + count)
        before, after = ((a0, b0), (a1, b1))[i // 2]
        total = own_ref[rows, :].astype(F32) + before[here, :].astype(F32) + after[here, :].astype(F32)
        mean = jnp.mean(total * total, axis=-1, keepdims=True)
        post = total * lax.rsqrt(mean + 1e-06) * gain
        row = lax.broadcasted_iota(jnp.int32, (count, 1), 0) + y * 128 + i * count
        out[rows, :] = jnp.where(row < length, rows_ref[rows, :].astype(F32) + post, 0.0).astype(BF16)
        pltpu.make_async_copy(out.at[rows], out_hbm.at[rows], osem).start()
    pltpu.make_async_copy(out, out_hbm, osem).wait()


def finish(scal, hidden, own, a0, a1, b0, b1, gain):
    width = hidden.shape[-1]
    return pl.pallas_call(
        finish_kernel,
        in_specs=[SMEM] + [VMEM] * 5 + [ANY] * 2,
        out_specs=ANY,
        out_shape=jax.ShapeDtypeStruct(hidden.shape, BF16),
        scratch_shapes=[
            pltpu.VMEM((64, width), BF16),
            pltpu.VMEM((64, width), BF16),
            pltpu.VMEM(hidden.shape, BF16),
            pltpu.SemaphoreType.DMA((2,)),
            pltpu.SemaphoreType.DMA,
        ],
        compiler_params=pltpu.CompilerParams(vmem_limit_bytes=SMALL_LIMIT),
        name="finish",
        cost_estimate=pl.CostEstimate(flops=6_000_000, bytes_accessed=7_000_000, transcendentals=128),
    )(scal, hidden, own, a1, b0, gain, a0, b1)


def angle_tables(maxlen):
    half = HD // 2
    freqs = 10000.0 ** (-jnp.arange(half, dtype=F32) / half)
    angles = jnp.arange(maxlen, dtype=jnp.int32).astype(F32)[:, None] * freqs[None, :]
    cosine, sine = jnp.cos(angles), jnp.sin(angles)
    return jnp.concatenate([cosine, cosine], -1), jnp.concatenate([-sine, sine], -1)


def torus(array, d, cores=(0, 1)):
    pairs = [
        (spot(z, x, c), spot(z + d[c][0], x + d[c][1], c))
        for z in range(NZ)
        for x in range(NX)
        for c in cores
    ]
    return lax.ppermute(array, "dp", pairs)


def one_way(array, source):
    pairs = [(spot(z, x, source), spot(z, x, 1 - source)) for z in range(NZ) for x in range(NX)]
    return lax.ppermute(array, "dp", pairs)


def swapped(array):
    return plane(array, dc=1)


SMALL_UP, SMALL_DOWN = ((1, 0), (0, 1)), ((-1, 0), (0, -1))
LARGE_UP, LARGE_DOWN = ((0, 1), (1, 0)), ((0, -1), (-1, 0))
NEAR, FAR = (0, -1, 1, -2), (2, -3, 3, 4)


def wrapped(dz, dx):
    return dz % NZ, dx % NX


PLACES_A = tuple(
    tuple(wrapped(dz, dx) for dz in zs)
    for zs, dx in ((NEAR, 0), (NEAR, -1), (NEAR, 1), (FAR, -1), (FAR, 1), (FAR, -2), (NEAR, 2), (FAR, 0))
)
PLACES_B = tuple(
    tuple(wrapped(dz, dx) for dx in NEAR) for dz in (0, -1, 1, -2, 2, -3, 3, -4)
)


def row_table(z, x, core):
    places = jnp.array([PLACES_A, PLACES_B], jnp.int32)
    rows = []
    for dc in range(2):
        owner = (core + dc) % 2
        mine = jnp.where(owner == 0, places[0], places[1])
        rows.append((((z + mine[..., 0]) % NZ * NX + (x + mine[..., 1]) % NX) * 2 + owner) * 72)
    return jnp.stack(rows).reshape(-1).astype(jnp.int32)


def gathered_weights(shard, core, tables):
    first = core == 0
    s1 = torus(shard, SMALL_UP)
    s2 = torus(shard, SMALL_DOWN)
    s3 = torus(s1, SMALL_UP)
    s4 = torus(s2, SMALL_DOWN)
    s5 = torus(s3, SMALL_UP)
    s6 = torus(s4, SMALL_DOWN)
    s7 = torus(s6, SMALL_DOWN)
    near = jnp.stack([shard, s1, s2, s3])
    r1 = torus(near, LARGE_UP)
    r2 = torus(near, LARGE_DOWN)
    r2, *angles = lax.optimization_barrier((r2, *tables[2:]))
    tables = (*tables[:2], *angles)
    far = jnp.stack([s4, s5, s6, s7])
    r3 = torus(jnp.where(first, far, r1), LARGE_UP)
    r4 = torus(jnp.where(first, far, r2), LARGE_DOWN)
    r5 = torus(r3, LARGE_UP)
    r6 = torus(jnp.where(first, *lax.optimization_barrier((r2, r4))), LARGE_DOWN)
    r7 = torus(r5[:2], LARGE_UP, (1,))
    r8 = torus(r6[2:], LARGE_DOWN, (1,))
    arrays = [near, r1, r2, r3, r4, r5, r6]
    others = [swapped(a) for a in arrays]
    far = far, one_way(far, 0)
    up = r7, one_way(r7, 1)
    down = r8, one_way(r8, 1)
    return arrays, others, far, up, down, tables


def layer(hidden, lengths, norm_gain, w_query, w_key, w_value, w_out, post_gain):
    _, local_len, width = hidden.shape
    hidden = hidden.reshape(local_len, width)
    place = lax.axis_index("dp")
    core = place % 2
    scal = jnp.stack([place // 8, (place // 2) % 4, core, lax.axis_index("mp"), lengths[0]]).astype(jnp.int32)
    shard = jnp.concatenate([w_query, w_key, w_value, w_out.T], axis=1)
    normed = normed_rows(hidden, norm_gain)
    above, below = column(normed, -1), column(normed, 1)
    across0 = column(above[:64], -1)
    across1 = column(below[64:], 1)
    tables = (scal, row_table(scal[0], scal[1], core), *angle_tables(local_len * NY))
    arrays, others, far, up, down, tables = gathered_weights(shard, core, tables)
    scal, table, cosine, sine = tables
    held = fill(scal, table, [normed], ((0, 0),), arrays[:1], (0,), (), (), width)
    held = fill(
        scal, table, [above, below], ((1, 0), (3, 0)), arrays[1:5] + others[:3],
        (1, 2, 3, 4, 8, 9, 10), far, held, width,
    )
    held = fill(
        scal, table, [across0, across1], ((2, 0), (2, 64)), arrays[5:] + others[3:5],
        (5, 6, 11, 12), (), held, width,
    )
    xbuf, wbuf = fill(scal, table, [], (), others[5:], (13, 14), (), held, width)
    rest = [up[0], down[0], up[1], down[1]]
    key, value, far0, far1, wbuf = project(scal, table, cosine, sine, rest, xbuf, wbuf)
    rfar0, rfar1 = column(far0, 1), column(far1, -1)
    up0, up1, down0, down1 = attend(scal, cosine, sine, key, value, xbuf, wbuf, (1, 3), (0, 64, 128, 192), 64)
    a1, b0 = column(up1, 1), column(down0, -1)
    (own,) = attend(scal, cosine, sine, key, value, xbuf, wbuf, (0,), (0,), 128)
    a0 = column((up0.astype(F32) + rfar0.astype(F32)).astype(BF16), 1)
    b1 = column((down1.astype(F32) + rfar1.astype(F32)).astype(BF16), -1)
    mixed = finish(scal, hidden, own, a0, a1, b0, b1, post_gain)
    return mixed[None], key[None], value[None]


def solution(mesh):
    return jax.shard_map(
        layer,
        mesh=mesh,
        in_specs=(
            P("dp", "mp", None),
            P("dp"),
            P(),
            P("dp", "mp"),
            P("dp", "mp"),
            P("dp", "mp"),
            P("mp", "dp"),
            P(),
        ),
        out_specs=(P("dp", "mp", None), P("dp", None, "mp"), P("dp", None, "mp")),
        check_vma=False,
    )
```

```python
import functools

import jax
import jax.numpy as jnp
from jax import lax
from jax.experimental import pallas as pl
from jax.experimental.pallas import tpu as pltpu
from jax.sharding import PartitionSpec as P


HD = 128
NZ, NX, NY = 8, 4, 4
F32 = jnp.float32
BF16 = jnp.bfloat16
ANY = pl.BlockSpec(memory_space=pl.ANY)
SMALL_LIMIT = 24 * 1024 * 1024


def spot(z, x, c):
    return ((z % NZ) * NX + (x % NX)) * 2 + c


def plane(array, dz=0, dx=0, dc=0):
    pairs = [
        (spot(z, x, c), spot(z + dz, x + dx, c ^ dc))
        for z in range(NZ)
        for x in range(NX)
        for c in range(2)
    ]
    return lax.ppermute(array, "dp", pairs)


def column(array, dy):
    return lax.ppermute(array, "mp", [(y, (y + dy) % NY) for y in range(NY)])


def norm_kernel(rows_ref, gain_ref, out_ref):
    rows = rows_ref[...].astype(F32)
    mean = jnp.mean(rows * rows, axis=-1, keepdims=True)
    out_ref[...] = (rows * lax.rsqrt(mean + 1e-06) * gain_ref[...]).astype(BF16)


def normed_rows(hidden, gain):
    rows, width = hidden.shape
    step = 64
    return pl.pallas_call(
        norm_kernel,
        grid=(rows // step,),
        in_specs=[
            pl.BlockSpec((step, width), lambda i: (i, 0)),
            pl.BlockSpec((width,), lambda i: (0,)),
        ],
        out_specs=pl.BlockSpec((step, width), lambda i: (i, 0)),
        out_shape=jax.ShapeDtypeStruct(hidden.shape, BF16),
        name="norm",
        cost_estimate=pl.CostEstimate(flops=2_000_000, bytes_accessed=2_400_000, transcendentals=128),
    )(hidden, gain)


def attended(scal, dy, q_ref, k_ref, v_ref, store):
    y, length = scal[3], scal[4]
    first = pl.multiple_of(lax.rem(y + dy, NY) * 128, 128)
    row = lax.broadcasted_iota(jnp.int32, (128, 512), 0) + first
    col = lax.broadcasted_iota(jnp.int32, (128, 512), 1)
    keep = (col <= row) & (col < length)
    for h in range(4):
        kv = slice((h // 2) * 128, (h // 2) * 128 + 128)
        score = lax.dot_general(
            q_ref[pl.ds(first, 128), h * 128 : h * 128 + 128],
            k_ref[:, kv],
            (((1,), (1,)), ((), ())),
            preferred_element_type=F32,
        )
        score = 50.0 * jnp.tanh(score * (1.0 / 50.0))
        score = jnp.where(keep, score, -1e30)
        top = jnp.max(score, axis=-1, keepdims=True)
        expo = jnp.exp(score - top)
        weights = (expo / jnp.sum(expo, axis=-1, keepdims=True)).astype(BF16)
        store(h, jnp.dot(weights, v_ref[:, kv], preferred_element_type=F32).astype(BF16))


def spread(att, wo, outs, width, chunk=1152):
    for at in range(0, width, chunk):
        partial = lax.dot_general(
            att[...], wo[at : at + chunk, :], (((1,), (1,)), ((), ())), preferred_element_type=F32
        )
        for ref, first in outs:
            ref[:, at : at + chunk] = partial[first : first + ref.shape[0]].astype(ref.dtype)


def start(pairs, sem):
    for src, dst in pairs:
        pltpu.make_async_copy(src, dst, sem).start()


def finished(target, rows, sem):
    part = target.at[pl.ds(0, rows)]
    pltpu.make_async_copy(part, part, sem).wait()


def rows_of(xbuf, y, dy, first, count):
    return xbuf.at[pl.ds(pl.multiple_of(lax.rem(y + dy, NY) * 128 + first, 64), count)]


def shards_of(ref, table, wbuf, base):
    for j in range(ref.shape[0]):
        yield ref.at[j], wbuf.at[pl.ds(pl.multiple_of(table[base + j], 8), 72)]


def fill_kernel(offsets, groups, n_old, scal, table, *refs):
    c, y = scal[2], scal[3]
    xs, refs = refs[: len(offsets)], refs[len(offsets) :]
    ws, refs = refs[: len(groups)], refs[len(groups) :]
    either, (xbuf, wbuf, sem) = refs[:-3][: -n_old or None], refs[-3:]

    for ref, at in zip(xs, offsets):
        pltpu.make_async_copy(ref, rows_of(xbuf, y, *at, ref.shape[0]), sem.at[0]).start()
    for ref, group in zip(ws, groups):
        start(shards_of(ref, table, wbuf, group * 4), sem.at[1])
    if either:
        for core, ref, base in ((0, either[0], 28), (1, either[1], 60)):

            @pl.when(c == core)
            def _():
                start(shards_of(ref, table, wbuf, base), sem.at[1])

    if xs:
        finished(xbuf, sum(ref.shape[0] for ref in xs), sem.at[0])
    finished(wbuf, 72 * 4 * (len(groups) + bool(either)), sem.at[1])


VMEM = pl.BlockSpec(memory_space=pltpu.VMEM)
SMEM = pl.BlockSpec(memory_space=pltpu.SMEM)


def fill(scal, table, xs, offsets, ws, groups, either, held, width):
    operands = [scal, table, *xs, *ws, *either, *held]
    n = len(operands)
    return pl.pallas_call(
        functools.partial(fill_kernel, offsets, groups, len(held)),
        in_specs=[SMEM] * 2 + [ANY] * (n - 2 - len(held)) + [VMEM] * len(held),
        out_specs=[VMEM] * 2,
        out_shape=[pltpu.VMEM((512, width), BF16), pltpu.VMEM((width, 1536), BF16)],
        scratch_shapes=[pltpu.SemaphoreType.DMA((2,))],
        input_output_aliases={n - 2: 0, n - 1: 1} if held else {},
        compiler_params=pltpu.CompilerParams(vmem_limit_bytes=SMALL_LIMIT),
        cost_estimate=pl.CostEstimate(flops=0, bytes_accessed=18_000_000, transcendentals=0),
    )(*operands)


def turned(raw, cos_ref, sin_ref, first, count):
    rows = pl.ds(first, count)
    return raw * cos_ref[rows, :] + pltpu.roll(raw, 64, 1) * sin_ref[rows, :]


def queries(scal, dy, xbuf, wbuf, cos_ref, sin_ref, q, slot):
    first = pl.multiple_of(lax.rem(scal[3] + dy, NY) * 128, 128)
    raw = jnp.dot(xbuf[pl.ds(first, 128), :], wbuf[:, 0:512], preferred_element_type=F32)
    for h in range(4):
        one = turned(raw[:, h * 128 : h * 128 + 128], cos_ref, sin_ref, first, 128)
        q[pl.ds(slot * 128, 128), h * 128 : h * 128 + 128] = (one * 144.0 ** (-0.5)).astype(BF16)


def attended(scal, dy, q, slot, k_ref, v_ref, att):
    y, length = scal[3], scal[4]
    first = lax.rem(y + dy, NY) * 128
    row = lax.broadcasted_iota(jnp.int32, (128, 512), 0) + first
    col = lax.broadcasted_iota(jnp.int32, (128, 512), 1)
    keep = (col <= row) & (col < length)
    mine = pl.ds(slot * 128, 128)
    for h in range(4):
        kv = slice((h // 2) * 128, (h // 2) * 128 + 128)
        head = slice(h * 128, h * 128 + 128)
        score = lax.dot_general(
            q[mine, head], k_ref[:, kv], (((1,), (1,)), ((), ())), preferred_element_type=F32
        )
        score = 50.0 * jnp.tanh(score * (1.0 / 50.0))
        score = jnp.where(keep, score, -1e30)
        top = jnp.max(score, axis=-1, keepdims=True)
        expo = jnp.exp(score - top)
        weights = (expo / jnp.sum(expo, axis=-1, keepdims=True)).astype(BF16)
        att[mine, head] = jnp.dot(weights, v_ref[:, kv], preferred_element_type=F32).astype(BF16)


def spread(att, wbuf, outs, chunk=1152):
    for at in range(0, wbuf.shape[0], chunk):
        partial = lax.dot_general(
            att[...], wbuf[at : at + chunk, 1024:1536], (((1,), (1,)), ((), ())), preferred_element_type=F32
        )
        for ref, first in outs:
            ref[:, at : at + chunk] = partial[first : first + ref.shape[0]].astype(ref.dtype)


def project_kernel(
    scal, table, cos_ref, sin_ref, up_own, down_own, up_other, down_other, xbuf, old,
    k_ref, v_ref, far0, far1, wbuf, q, att, sem,
):
    c, length = scal[2], scal[4]

    for core, halves, base in ((0, (up_other, down_other), 60), (1, (up_own, down_own), 28)):

        @pl.when(c == core)
        def _():
            for i, ref in enumerate(halves):
                start(shards_of(ref, table, wbuf, base + 2 * i), sem)

    finished(wbuf, 72 * 4, sem)
    live = lax.broadcasted_iota(jnp.int32, (512, 128), 0) < length
    raw = jnp.dot(xbuf[...], wbuf[:, 512:768], preferred_element_type=F32)
    for h in range(2):
        head = slice(h * 128, h * 128 + 128)
        k_ref[:, head] = jnp.where(live, turned(raw[:, head], cos_ref, sin_ref, 0, 512), 0.0).astype(BF16)
    raw = jnp.dot(xbuf[...], wbuf[:, 768:1024], preferred_element_type=F32)
    for h in range(2):
        head = slice(h * 128, h * 128 + 128)
        v_ref[:, head] = jnp.where(live, raw[:, head], 0.0).astype(BF16)
    queries(scal, 2, xbuf, wbuf, cos_ref, sin_ref, q, 0)
    attended(scal, 2, q, 0, k_ref, v_ref, att)
    spread(att, wbuf, ((far0, 0), (far1, 64)))


def project(scal, table, cosine, sine, arrays, xbuf, wbuf):
    width = wbuf.shape[0]
    outs = [(512, 256), (512, 256), (64, width), (64, width)]
    n = 4 + len(arrays)
    return pl.pallas_call(
        project_kernel,
        in_specs=[SMEM] * 2 + [VMEM] * 2 + [ANY] * len(arrays) + [VMEM] * 2,
        out_specs=[VMEM] * 5,
        out_shape=[jax.ShapeDtypeStruct(shape, BF16) for shape in outs] + [pltpu.VMEM(wbuf.shape, BF16)],
        scratch_shapes=[
            pltpu.VMEM((128, 512), BF16),
            pltpu.VMEM((128, 512), BF16),
            pltpu.SemaphoreType.DMA,
        ],
        input_output_aliases={n + 1: 4},
        compiler_params=pltpu.CompilerParams(vmem_limit_bytes=SMALL_LIMIT),
        name="project",
        cost_estimate=pl.CostEstimate(flops=4_000_000_000, bytes_accessed=10_000_000, transcendentals=524_288),
    )(scal, table, cosine, sine, *arrays, xbuf, wbuf)


def attend_kernel(blocks, outs, scal, cos_ref, sin_ref, k_ref, v_ref, xbuf, wbuf, *refs):
    out_refs, (q, att) = refs[:-2], refs[-2:]
    stride = blocks[-1] - blocks[0]

    def block(slot, carry):
        dy = blocks[0] + slot * stride
        queries(scal, dy, xbuf, wbuf, cos_ref, sin_ref, q, slot)
        attended(scal, dy, q, slot, k_ref, v_ref, att)
        return carry

    lax.fori_loop(0, len(blocks), block, 0)
    chunk = 1152

    def stretch(i, carry):
        at = pl.multiple_of(i * chunk, 128)
        partial = lax.dot_general(
            att[...], wbuf[pl.ds(at, chunk), 1024:1536], (((1,), (1,)), ((), ())), preferred_element_type=F32
        )
        for ref, first in zip(out_refs, outs):
            ref[:, pl.ds(at, chunk)] = partial[first : first + ref.shape[0]].astype(ref.dtype)
        return carry

    lax.fori_loop(0, wbuf.shape[0] // chunk, stretch, 0)


def attend(scal, cosine, sine, key, value, xbuf, wbuf, blocks, outs, count):
    width = wbuf.shape[0]
    n = len(blocks)
    return pl.pallas_call(
        functools.partial(attend_kernel, blocks, outs),
        in_specs=[SMEM] + [VMEM] * 6,
        out_specs=[VMEM] * len(outs),
        out_shape=[jax.ShapeDtypeStruct((count, width), BF16)] * len(outs),
        scratch_shapes=[pltpu.VMEM((n * 128, 512), BF16)] * 2,
        compiler_params=pltpu.CompilerParams(vmem_limit_bytes=SMALL_LIMIT),
        cost_estimate=pl.CostEstimate(
            flops=n * 1_400_000_000, bytes_accessed=1_000_000 + n * 1_200_000, transcendentals=n * 524_288
        ),
    )(scal, cosine, sine, key, value, xbuf, wbuf)


def finish_kernel(scal, rows_ref, own_ref, a1, b0, gain_ref, a0_hbm, b1_hbm, out_hbm, a0, b1, out, sem, osem):
    y, length = scal[3], scal[4]
    first = pltpu.make_async_copy(a0_hbm, a0, sem.at[0])
    second = pltpu.make_async_copy(b1_hbm, b1, sem.at[1])
    first.start()
    second.start()
    gain = gain_ref[...]
    count = 32
    for i in range(4):
        if i % 2 == 0:
            (first, second)[i // 2].wait()
        rows = slice(i * count, i * count + count)
        here = slice(i % 2 * count, i % 2 * count + count)
        before, after = ((a0, b0), (a1, b1))[i // 2]
        total = own_ref[rows, :].astype(F32) + before[here, :].astype(F32) + after[here, :].astype(F32)
        mean = jnp.mean(total * total, axis=-1, keepdims=True)
        post = total * lax.rsqrt(mean + 1e-06) * gain
        row = lax.broadcasted_iota(jnp.int32, (count, 1), 0) + y * 128 + i * count
        out[rows, :] = jnp.where(row < length, rows_ref[rows, :].astype(F32) + post, 0.0).astype(BF16)
        pltpu.make_async_copy(out.at[rows], out_hbm.at[rows], osem).start()
    pltpu.make_async_copy(out, out_hbm, osem).wait()


def finish(scal, hidden, own, a0, a1, b0, b1, gain):
    width = hidden.shape[-1]
    return pl.pallas_call(
        finish_kernel,
        in_specs=[SMEM] + [VMEM] * 5 + [ANY] * 2,
        out_specs=ANY,
        out_shape=jax.ShapeDtypeStruct(hidden.shape, BF16),
        scratch_shapes=[
            pltpu.VMEM((64, width), BF16),
            pltpu.VMEM((64, width), BF16),
            pltpu.VMEM(hidden.shape, BF16),
            pltpu.SemaphoreType.DMA((2,)),
            pltpu.SemaphoreType.DMA,
        ],
        compiler_params=pltpu.CompilerParams(vmem_limit_bytes=SMALL_LIMIT),
        name="finish",
        cost_estimate=pl.CostEstimate(flops=6_000_000, bytes_accessed=7_000_000, transcendentals=128),
    )(scal, hidden, own, a1, b0, gain, a0, b1)


def angle_tables(maxlen):
    half = HD // 2
    freqs = 10000.0 ** (-jnp.arange(half, dtype=F32) / half)
    angles = jnp.arange(maxlen, dtype=jnp.int32).astype(F32)[:, None] * freqs[None, :]
    cosine, sine = jnp.cos(angles), jnp.sin(angles)
    return jnp.concatenate([cosine, cosine], -1), jnp.concatenate([-sine, sine], -1)


def torus(array, d, cores=(0, 1)):
    pairs = [
        (spot(z, x, c), spot(z + d[c][0], x + d[c][1], c))
        for z in range(NZ)
        for x in range(NX)
        for c in cores
    ]
    return lax.ppermute(array, "dp", pairs)


def one_way(array, source):
    pairs = [(spot(z, x, source), spot(z, x, 1 - source)) for z in range(NZ) for x in range(NX)]
    return lax.ppermute(array, "dp", pairs)


def swapped(array):
    return plane(array, dc=1)


SMALL_UP, SMALL_DOWN = ((1, 0), (0, 1)), ((-1, 0), (0, -1))
LARGE_UP, LARGE_DOWN = ((0, 1), (1, 0)), ((0, -1), (-1, 0))
NEAR, FAR = (0, -1, 1, -2), (2, -3, 3, 4)


def wrapped(dz, dx):
    return dz % NZ, dx % NX


PLACES_A = tuple(
    tuple(wrapped(dz, dx) for dz in zs)
    for zs, dx in ((NEAR, 0), (NEAR, -1), (NEAR, 1), (FAR, -1), (FAR, 1), (FAR, -2), (NEAR, 2), (FAR, 0))
)
PLACES_B = tuple(
    tuple(wrapped(dz, dx) for dx in NEAR) for dz in (0, -1, 1, -2, 2, -3, 3, -4)
)


def row_table(z, x, core):
    places = jnp.array([PLACES_A, PLACES_B], jnp.int32)
    rows = []
    for dc in range(2):
        owner = (core + dc) % 2
        mine = jnp.where(owner == 0, places[0], places[1])
        rows.append((((z + mine[..., 0]) % NZ * NX + (x + mine[..., 1]) % NX) * 2 + owner) * 72)
    return jnp.stack(rows).reshape(-1).astype(jnp.int32)


def gathered_weights(shard, core, tables):
    first = core == 0
    s1 = torus(shard, SMALL_UP)
    s2 = torus(shard, SMALL_DOWN)
    s3 = torus(s1, SMALL_UP)
    s4 = torus(s2, SMALL_DOWN)
    s5 = torus(s3, SMALL_UP)
    s6 = torus(s4, SMALL_DOWN)
    s7 = torus(s6, SMALL_DOWN)
    near = jnp.stack([shard, s1, s2, s3])
    r1 = torus(near, LARGE_UP)
    r2 = torus(near, LARGE_DOWN)
    r2, tables = lax.optimization_barrier((r2, tables))
    far = jnp.stack([s4, s5, s6, s7])
    r3 = torus(jnp.where(first, far, r1), LARGE_UP)
    r4 = torus(jnp.where(first, far, r2), LARGE_DOWN)
    r5 = torus(r3, LARGE_UP)
    r6 = torus(jnp.where(first, *lax.optimization_barrier((r2, r4))), LARGE_DOWN)
    r7 = torus(r5[:2], LARGE_UP, (1,))
    r8 = torus(r6[2:], LARGE_DOWN, (1,))
    arrays = [near, r1, r2, r3, r4, r5, r6]
    others = [swapped(a) for a in arrays]
    far = far, one_way(far, 0)
    up = r7, one_way(r7, 1)
    down = r8, one_way(r8, 1)
    return arrays, others, far, up, down, tables


def layer(hidden, lengths, norm_gain, w_query, w_key, w_value, w_out, post_gain):
    _, local_len, width = hidden.shape
    hidden = hidden.reshape(local_len, width)
    place = lax.axis_index("dp")
    core = place % 2
    scal = jnp.stack([place // 8, (place // 2) % 4, core, lax.axis_index("mp"), lengths[0]]).astype(jnp.int32)
    shard = jnp.concatenate([w_query, w_key, w_value, w_out.T], axis=1)
    normed = normed_rows(hidden, norm_gain)
    above, below = column(normed, -1), column(normed, 1)
    across0 = column(above[:64], -1)
    across1 = column(below[64:], 1)
    tables = (scal, row_table(scal[0], scal[1], core), *angle_tables(local_len * NY))
    arrays, others, far, up, down, tables = gathered_weights(shard, core, tables)
    scal, table, cosine, sine = tables
    held = fill(
        scal, table, [normed, above, below], ((0, 0), (1, 0), (3, 0)), arrays[:5] + others[:3],
        (0, 1, 2, 3, 4, 8, 9, 10), far, (), width,
    )
    held = fill(
        scal, table, [across0, across1], ((2, 0), (2, 64)), arrays[5:] + others[3:5],
        (5, 6, 11, 12), (), held, width,
    )
    xbuf, wbuf = fill(scal, table, [], (), others[5:], (13, 14), (), held, width)
    rest = [up[0], down[0], up[1], down[1]]
    key, value, far0, far1, wbuf = project(scal, table, cosine, sine, rest, xbuf, wbuf)
    rfar0, rfar1 = column(far0, 1), column(far1, -1)
    up0, up1, down0, down1 = attend(scal, cosine, sine, key, value, xbuf, wbuf, (1, 3), (0, 64, 128, 192), 64)
    a1, b0 = column(up1, 1), column(down0, -1)
    (own,) = attend(scal, cosine, sine, key, value, xbuf, wbuf, (0,), (0,), 128)
    a0 = column((up0.astype(F32) + rfar0.astype(F32)).astype(BF16), 1)
    b1 = column((down1.astype(F32) + rfar1.astype(F32)).astype(BF16), -1)
    mixed = finish(scal, hidden, own, a0, a1, b0, b1, post_gain)
    return mixed[None], key[None], value[None]


def solution(mesh):
    return jax.shard_map(
        layer,
        mesh=mesh,
        in_specs=(
            P("dp", "mp", None),
            P("dp"),
            P(),
            P("dp", "mp"),
            P("dp", "mp"),
            P("dp", "mp"),
            P("mp", "dp"),
            P(),
        ),
        out_specs=(P("dp", "mp", None), P("dp", None, "mp"), P("dp", None, "mp")),
        check_vma=False,
    )
```

```python
import functools

import jax
import jax.numpy as jnp
from jax import lax
from jax.experimental import pallas as pl
from jax.experimental.pallas import tpu as pltpu
from jax.sharding import PartitionSpec as P


HD = 128
NZ, NX, NY = 8, 4, 4
F32 = jnp.float32
BF16 = jnp.bfloat16
ANY = pl.BlockSpec(memory_space=pl.ANY)
SMALL_LIMIT = 24 * 1024 * 1024


def spot(z, x, c):
    return ((z % NZ) * NX + (x % NX)) * 2 + c


def plane(array, dz=0, dx=0, dc=0):
    pairs = [
        (spot(z, x, c), spot(z + dz, x + dx, c ^ dc))
        for z in range(NZ)
        for x in range(NX)
        for c in range(2)
    ]
    return lax.ppermute(array, "dp", pairs)


def column(array, dy):
    return lax.ppermute(array, "mp", [(y, (y + dy) % NY) for y in range(NY)])


def norm_kernel(rows_ref, gain_ref, out_ref):
    rows = rows_ref[...].astype(F32)
    mean = jnp.mean(rows * rows, axis=-1, keepdims=True)
    out_ref[...] = (rows * lax.rsqrt(mean + 1e-06) * gain_ref[...]).astype(BF16)


def normed_rows(hidden, gain):
    rows, width = hidden.shape
    step = 64
    return pl.pallas_call(
        norm_kernel,
        grid=(rows // step,),
        in_specs=[
            pl.BlockSpec((step, width), lambda i: (i, 0)),
            pl.BlockSpec((width,), lambda i: (0,)),
        ],
        out_specs=pl.BlockSpec((step, width), lambda i: (i, 0)),
        out_shape=jax.ShapeDtypeStruct(hidden.shape, BF16),
        name="norm",
        cost_estimate=pl.CostEstimate(flops=2_000_000, bytes_accessed=2_400_000, transcendentals=128),
    )(hidden, gain)


def attended(scal, dy, q_ref, k_ref, v_ref, store):
    y, length = scal[3], scal[4]
    first = pl.multiple_of(lax.rem(y + dy, NY) * 128, 128)
    row = lax.broadcasted_iota(jnp.int32, (128, 512), 0) + first
    col = lax.broadcasted_iota(jnp.int32, (128, 512), 1)
    keep = (col <= row) & (col < length)
    for h in range(4):
        kv = slice((h // 2) * 128, (h // 2) * 128 + 128)
        score = lax.dot_general(
            q_ref[pl.ds(first, 128), h * 128 : h * 128 + 128],
            k_ref[:, kv],
            (((1,), (1,)), ((), ())),
            preferred_element_type=F32,
        )
        score = 50.0 * jnp.tanh(score * (1.0 / 50.0))
        score = jnp.where(keep, score, -1e30)
        top = jnp.max(score, axis=-1, keepdims=True)
        expo = jnp.exp(score - top)
        weights = (expo / jnp.sum(expo, axis=-1, keepdims=True)).astype(BF16)
        store(h, jnp.dot(weights, v_ref[:, kv], preferred_element_type=F32).astype(BF16))


def spread(att, wo, outs, width, chunk=1152):
    for at in range(0, width, chunk):
        partial = lax.dot_general(
            att[...], wo[at : at + chunk, :], (((1,), (1,)), ((), ())), preferred_element_type=F32
        )
        for ref, first in outs:
            ref[:, at : at + chunk] = partial[first : first + ref.shape[0]].astype(ref.dtype)


def start(pairs, sem):
    for src, dst in pairs:
        half = src.shape[-1] // 2
        for part in range(2):
            cols = pl.ds(part * half, half)
            pltpu.make_async_copy(src.at[:, cols], dst.at[:, cols], sem).start()


def finished(target, rows, sem):
    part = target.at[pl.ds(0, rows)]
    pltpu.make_async_copy(part, part, sem).wait()


def rows_of(xbuf, y, dy, first, count):
    return xbuf.at[pl.ds(pl.multiple_of(lax.rem(y + dy, NY) * 128 + first, 64), count)]


def shards_of(ref, table, wbuf, base):
    for j in range(ref.shape[0]):
        yield ref.at[j], wbuf.at[pl.ds(pl.multiple_of(table[base + j], 8), 72)]


def fill_kernel(offsets, groups, n_old, scal, table, *refs):
    c, y = scal[2], scal[3]
    xs, refs = refs[: len(offsets)], refs[len(offsets) :]
    ws, refs = refs[: len(groups)], refs[len(groups) :]
    either, (xbuf, wbuf, sem) = refs[:-3][: -n_old or None], refs[-3:]

    start([(ref, rows_of(xbuf, y, *at, ref.shape[0])) for ref, at in zip(xs, offsets)], sem.at[0])
    for ref, group in zip(ws, groups):
        start(shards_of(ref, table, wbuf, group * 4), sem.at[1])
    if either:
        for core, ref, base in ((0, either[0], 28), (1, either[1], 60)):

            @pl.when(c == core)
            def _():
                start(shards_of(ref, table, wbuf, base), sem.at[1])

    if xs:
        finished(xbuf, sum(ref.shape[0] for ref in xs), sem.at[0])
    finished(wbuf, 72 * 4 * (len(groups) + bool(either)), sem.at[1])


VMEM = pl.BlockSpec(memory_space=pltpu.VMEM)
SMEM = pl.BlockSpec(memory_space=pltpu.SMEM)


def fill(scal, table, xs, offsets, ws, groups, either, held, width):
    operands = [scal, table, *xs, *ws, *either, *held]
    n = len(operands)
    return pl.pallas_call(
        functools.partial(fill_kernel, offsets, groups, len(held)),
        in_specs=[SMEM] * 2 + [ANY] * (n - 2 - len(held)) + [VMEM] * len(held),
        out_specs=[VMEM] * 2,
        out_shape=[pltpu.VMEM((512, width), BF16), pltpu.VMEM((width, 1536), BF16)],
        scratch_shapes=[pltpu.SemaphoreType.DMA((2,))],
        input_output_aliases={n - 2: 0, n - 1: 1} if held else {},
        compiler_params=pltpu.CompilerParams(vmem_limit_bytes=SMALL_LIMIT),
        cost_estimate=pl.CostEstimate(flops=0, bytes_accessed=18_000_000, transcendentals=0),
    )(*operands)


def turned(raw, cos_ref, sin_ref, first, count):
    rows = pl.ds(first, count)
    return raw * cos_ref[rows, :] + pltpu.roll(raw, 64, 1) * sin_ref[rows, :]


def queries(scal, dy, xbuf, wbuf, cos_ref, sin_ref, q, slot):
    first = pl.multiple_of(lax.rem(scal[3] + dy, NY) * 128, 128)
    raw = jnp.dot(xbuf[pl.ds(first, 128), :], wbuf[:, 0:512], preferred_element_type=F32)
    for h in range(4):
        one = turned(raw[:, h * 128 : h * 128 + 128], cos_ref, sin_ref, first, 128)
        q[pl.ds(slot * 128, 128), h * 128 : h * 128 + 128] = (one * 144.0 ** (-0.5)).astype(BF16)


def attended(scal, dy, q, slot, k_ref, v_ref, att):
    y, length = scal[3], scal[4]
    first = lax.rem(y + dy, NY) * 128
    row = lax.broadcasted_iota(jnp.int32, (128, 512), 0) + first
    col = lax.broadcasted_iota(jnp.int32, (128, 512), 1)
    keep = (col <= row) & (col < length)
    mine = pl.ds(slot * 128, 128)
    for h in range(4):
        kv = slice((h // 2) * 128, (h // 2) * 128 + 128)
        head = slice(h * 128, h * 128 + 128)
        score = lax.dot_general(
            q[mine, head], k_ref[:, kv], (((1,), (1,)), ((), ())), preferred_element_type=F32
        )
        score = 50.0 * jnp.tanh(score * (1.0 / 50.0))
        score = jnp.where(keep, score, -1e30)
        top = jnp.max(score, axis=-1, keepdims=True)
        expo = jnp.exp(score - top)
        weights = (expo / jnp.sum(expo, axis=-1, keepdims=True)).astype(BF16)
        att[mine, head] = jnp.dot(weights, v_ref[:, kv], preferred_element_type=F32).astype(BF16)


def spread(att, wbuf, outs, chunk=1152):
    for at in range(0, wbuf.shape[0], chunk):
        partial = lax.dot_general(
            att[...], wbuf[at : at + chunk, 1024:1536], (((1,), (1,)), ((), ())), preferred_element_type=F32
        )
        for ref, first in outs:
            ref[:, at : at + chunk] = partial[first : first + ref.shape[0]].astype(ref.dtype)


def project_kernel(
    scal, table, cos_ref, sin_ref, up_own, down_own, up_other, down_other, xbuf, old,
    k_ref, v_ref, far0, far1, wbuf, q, att, sem,
):
    c, length = scal[2], scal[4]

    for core, halves, base in ((0, (up_other, down_other), 60), (1, (up_own, down_own), 28)):

        @pl.when(c == core)
        def _():
            for i, ref in enumerate(halves):
                start(shards_of(ref, table, wbuf, base + 2 * i), sem)

    finished(wbuf, 72 * 4, sem)
    live = lax.broadcasted_iota(jnp.int32, (512, 128), 0) < length
    raw = jnp.dot(xbuf[...], wbuf[:, 512:768], preferred_element_type=F32)
    for h in range(2):
        head = slice(h * 128, h * 128 + 128)
        k_ref[:, head] = jnp.where(live, turned(raw[:, head], cos_ref, sin_ref, 0, 512), 0.0).astype(BF16)
    raw = jnp.dot(xbuf[...], wbuf[:, 768:1024], preferred_element_type=F32)
    for h in range(2):
        head = slice(h * 128, h * 128 + 128)
        v_ref[:, head] = jnp.where(live, raw[:, head], 0.0).astype(BF16)
    queries(scal, 2, xbuf, wbuf, cos_ref, sin_ref, q, 0)
    attended(scal, 2, q, 0, k_ref, v_ref, att)
    spread(att, wbuf, ((far0, 0), (far1, 64)))


def project(scal, table, cosine, sine, arrays, xbuf, wbuf):
    width = wbuf.shape[0]
    outs = [(512, 256), (512, 256), (64, width), (64, width)]
    n = 4 + len(arrays)
    return pl.pallas_call(
        project_kernel,
        in_specs=[SMEM] * 2 + [VMEM] * 2 + [ANY] * len(arrays) + [VMEM] * 2,
        out_specs=[VMEM] * 5,
        out_shape=[jax.ShapeDtypeStruct(shape, BF16) for shape in outs] + [pltpu.VMEM(wbuf.shape, BF16)],
        scratch_shapes=[
            pltpu.VMEM((128, 512), BF16),
            pltpu.VMEM((128, 512), BF16),
            pltpu.SemaphoreType.DMA,
        ],
        input_output_aliases={n + 1: 4},
        compiler_params=pltpu.CompilerParams(vmem_limit_bytes=SMALL_LIMIT),
        name="project",
        cost_estimate=pl.CostEstimate(flops=4_000_000_000, bytes_accessed=10_000_000, transcendentals=524_288),
    )(scal, table, cosine, sine, *arrays, xbuf, wbuf)


def attend_kernel(blocks, outs, scal, cos_ref, sin_ref, k_ref, v_ref, xbuf, wbuf, *refs):
    out_refs, (q, att) = refs[:-2], refs[-2:]
    stride = blocks[-1] - blocks[0]

    def block(slot, carry):
        dy = blocks[0] + slot * stride
        queries(scal, dy, xbuf, wbuf, cos_ref, sin_ref, q, slot)
        attended(scal, dy, q, slot, k_ref, v_ref, att)
        return carry

    lax.fori_loop(0, len(blocks), block, 0)
    chunk = 1152

    def stretch(i, carry):
        at = pl.multiple_of(i * chunk, 128)
        partial = lax.dot_general(
            att[...], wbuf[pl.ds(at, chunk), 1024:1536], (((1,), (1,)), ((), ())), preferred_element_type=F32
        )
        for ref, first in zip(out_refs, outs):
            ref[:, pl.ds(at, chunk)] = partial[first : first + ref.shape[0]].astype(ref.dtype)
        return carry

    lax.fori_loop(0, wbuf.shape[0] // chunk, stretch, 0)


def attend(scal, cosine, sine, key, value, xbuf, wbuf, blocks, outs, count):
    width = wbuf.shape[0]
    n = len(blocks)
    return pl.pallas_call(
        functools.partial(attend_kernel, blocks, outs),
        in_specs=[SMEM] + [VMEM] * 6,
        out_specs=[VMEM] * len(outs),
        out_shape=[jax.ShapeDtypeStruct((count, width), BF16)] * len(outs),
        scratch_shapes=[pltpu.VMEM((n * 128, 512), BF16)] * 2,
        compiler_params=pltpu.CompilerParams(vmem_limit_bytes=SMALL_LIMIT),
        cost_estimate=pl.CostEstimate(
            flops=n * 1_400_000_000, bytes_accessed=1_000_000 + n * 1_200_000, transcendentals=n * 524_288
        ),
    )(scal, cosine, sine, key, value, xbuf, wbuf)


def finish_kernel(scal, rows_ref, own_ref, a1, b0, gain_ref, a0_hbm, b1_hbm, out_hbm, a0, b1, out, sem, osem):
    y, length = scal[3], scal[4]
    first = pltpu.make_async_copy(a0_hbm, a0, sem.at[0])
    second = pltpu.make_async_copy(b1_hbm, b1, sem.at[1])
    start([(a0_hbm, a0)], sem.at[0])
    start([(b1_hbm, b1)], sem.at[1])
    gain = gain_ref[...]
    count = 32
    for i in range(4):
        if i % 2 == 0:
            (first, second)[i // 2].wait()
        rows = slice(i * count, i * count + count)
        here = slice(i % 2 * count, i % 2 * count + count)
        before, after = ((a0, b0), (a1, b1))[i // 2]
        total = own_ref[rows, :].astype(F32) + before[here, :].astype(F32) + after[here, :].astype(F32)
        mean = jnp.mean(total * total, axis=-1, keepdims=True)
        post = total * lax.rsqrt(mean + 1e-06) * gain
        row = lax.broadcasted_iota(jnp.int32, (count, 1), 0) + y * 128 + i * count
        out[rows, :] = jnp.where(row < length, rows_ref[rows, :].astype(F32) + post, 0.0).astype(BF16)
        start([(out.at[rows], out_hbm.at[rows])], osem)
    pltpu.make_async_copy(out, out_hbm, osem).wait()


def finish(scal, hidden, own, a0, a1, b0, b1, gain):
    width = hidden.shape[-1]
    return pl.pallas_call(
        finish_kernel,
        in_specs=[SMEM] + [VMEM] * 5 + [ANY] * 2,
        out_specs=ANY,
        out_shape=jax.ShapeDtypeStruct(hidden.shape, BF16),
        scratch_shapes=[
            pltpu.VMEM((64, width), BF16),
            pltpu.VMEM((64, width), BF16),
            pltpu.VMEM(hidden.shape, BF16),
            pltpu.SemaphoreType.DMA((2,)),
            pltpu.SemaphoreType.DMA,
        ],
        compiler_params=pltpu.CompilerParams(vmem_limit_bytes=SMALL_LIMIT),
        name="finish",
        cost_estimate=pl.CostEstimate(flops=6_000_000, bytes_accessed=7_000_000, transcendentals=128),
    )(scal, hidden, own, a1, b0, gain, a0, b1)


def angle_tables(maxlen):
    half = HD // 2
    freqs = 10000.0 ** (-jnp.arange(half, dtype=F32) / half)
    angles = jnp.arange(maxlen, dtype=jnp.int32).astype(F32)[:, None] * freqs[None, :]
    cosine, sine = jnp.cos(angles), jnp.sin(angles)
    return jnp.concatenate([cosine, cosine], -1), jnp.concatenate([-sine, sine], -1)


def torus(array, d, cores=(0, 1)):
    pairs = [
        (spot(z, x, c), spot(z + d[c][0], x + d[c][1], c))
        for z in range(NZ)
        for x in range(NX)
        for c in cores
    ]
    return lax.ppermute(array, "dp", pairs)


def one_way(array, source):
    pairs = [(spot(z, x, source), spot(z, x, 1 - source)) for z in range(NZ) for x in range(NX)]
    return lax.ppermute(array, "dp", pairs)


def swapped(array):
    return plane(array, dc=1)


SMALL_UP, SMALL_DOWN = ((1, 0), (0, 1)), ((-1, 0), (0, -1))
LARGE_UP, LARGE_DOWN = ((0, 1), (1, 0)), ((0, -1), (-1, 0))
NEAR, FAR = (0, -1, 1, -2), (2, -3, 3, 4)


def wrapped(dz, dx):
    return dz % NZ, dx % NX


PLACES_A = tuple(
    tuple(wrapped(dz, dx) for dz in zs)
    for zs, dx in ((NEAR, 0), (NEAR, -1), (NEAR, 1), (FAR, -1), (FAR, 1), (FAR, -2), (NEAR, 2), (FAR, 0))
)
PLACES_B = tuple(
    tuple(wrapped(dz, dx) for dx in NEAR) for dz in (0, -1, 1, -2, 2, -3, 3, -4)
)


def row_table(z, x, core):
    places = jnp.array([PLACES_A, PLACES_B], jnp.int32)
    rows = []
    for dc in range(2):
        owner = (core + dc) % 2
        mine = jnp.where(owner == 0, places[0], places[1])
        rows.append((((z + mine[..., 0]) % NZ * NX + (x + mine[..., 1]) % NX) * 2 + owner) * 72)
    return jnp.stack(rows).reshape(-1).astype(jnp.int32)


def gathered_weights(shard, core, tables):
    first = core == 0
    s1 = torus(shard, SMALL_UP)
    s2 = torus(shard, SMALL_DOWN)
    s3 = torus(s1, SMALL_UP)
    s4 = torus(s2, SMALL_DOWN)
    s5 = torus(s3, SMALL_UP)
    s6 = torus(s4, SMALL_DOWN)
    s7 = torus(s6, SMALL_DOWN)
    near = jnp.stack([shard, s1, s2, s3])
    r1 = torus(near, LARGE_UP)
    r2 = torus(near, LARGE_DOWN)
    r2, tables = lax.optimization_barrier((r2, tables))
    far = jnp.stack([s4, s5, s6, s7])
    r3 = torus(jnp.where(first, far, r1), LARGE_UP)
    r4 = torus(jnp.where(first, far, r2), LARGE_DOWN)
    r5 = torus(r3, LARGE_UP)
    r6 = torus(jnp.where(first, *lax.optimization_barrier((r2, r4))), LARGE_DOWN)
    r7 = torus(r5[:2], LARGE_UP, (1,))
    r8 = torus(r6[2:], LARGE_DOWN, (1,))
    arrays = [near, r1, r2, r3, r4, r5, r6]
    others = [swapped(a) for a in arrays]
    far = far, one_way(far, 0)
    up = r7, one_way(r7, 1)
    down = r8, one_way(r8, 1)
    return arrays, others, far, up, down, tables


def layer(hidden, lengths, norm_gain, w_query, w_key, w_value, w_out, post_gain):
    _, local_len, width = hidden.shape
    hidden = hidden.reshape(local_len, width)
    place = lax.axis_index("dp")
    core = place % 2
    scal = jnp.stack([place // 8, (place // 2) % 4, core, lax.axis_index("mp"), lengths[0]]).astype(jnp.int32)
    shard = jnp.concatenate([w_query, w_key, w_value, w_out.T], axis=1)
    normed = normed_rows(hidden, norm_gain)
    above, below = column(normed, -1), column(normed, 1)
    across0 = column(above[:64], -1)
    across1 = column(below[64:], 1)
    tables = (scal, row_table(scal[0], scal[1], core), *angle_tables(local_len * NY))
    arrays, others, far, up, down, tables = gathered_weights(shard, core, tables)
    scal, table, cosine, sine = tables
    held = fill(
        scal, table, [normed, above, below], ((0, 0), (1, 0), (3, 0)), arrays[:5] + others[:3],
        (0, 1, 2, 3, 4, 8, 9, 10), far, (), width,
    )
    held = fill(
        scal, table, [across0, across1], ((2, 0), (2, 64)), arrays[5:] + others[3:5],
        (5, 6, 11, 12), (), held, width,
    )
    xbuf, wbuf = fill(scal, table, [], (), others[5:], (13, 14), (), held, width)
    rest = [up[0], down[0], up[1], down[1]]
    key, value, far0, far1, wbuf = project(scal, table, cosine, sine, rest, xbuf, wbuf)
    rfar0, rfar1 = column(far0, 1), column(far1, -1)
    up0, up1, down0, down1 = attend(scal, cosine, sine, key, value, xbuf, wbuf, (1, 3), (0, 64, 128, 192), 64)
    a1, b0 = column(up1, 1), column(down0, -1)
    (own,) = attend(scal, cosine, sine, key, value, xbuf, wbuf, (0,), (0,), 128)
    a0 = column((up0.astype(F32) + rfar0.astype(F32)).astype(BF16), 1)
    b1 = column((down1.astype(F32) + rfar1.astype(F32)).astype(BF16), -1)
    mixed = finish(scal, hidden, own, a0, a1, b0, b1, post_gain)
    return mixed[None], key[None], value[None]


def solution(mesh):
    return jax.shard_map(
        layer,
        mesh=mesh,
        in_specs=(
            P("dp", "mp", None),
            P("dp"),
            P(),
            P("dp", "mp"),
            P("dp", "mp"),
            P("dp", "mp"),
            P("mp", "dp"),
            P(),
        ),
        out_specs=(P("dp", "mp", None), P("dp", None, "mp"), P("dp", None, "mp")),
        check_vma=False,
    )
```

```python
import functools

import jax
import jax.numpy as jnp
from jax import lax
from jax.experimental import pallas as pl
from jax.experimental.pallas import tpu as pltpu
from jax.sharding import PartitionSpec as P


HD = 128
NZ, NX, NY = 8, 4, 4
F32 = jnp.float32
BF16 = jnp.bfloat16
ANY = pl.BlockSpec(memory_space=pl.ANY)
SMALL_LIMIT = 24 * 1024 * 1024


def spot(z, x, c):
    return ((z % NZ) * NX + (x % NX)) * 2 + c


def plane(array, dz=0, dx=0, dc=0):
    pairs = [
        (spot(z, x, c), spot(z + dz, x + dx, c ^ dc))
        for z in range(NZ)
        for x in range(NX)
        for c in range(2)
    ]
    return lax.ppermute(array, "dp", pairs)


def column(array, dy):
    return lax.ppermute(array, "mp", [(y, (y + dy) % NY) for y in range(NY)])


def norm_kernel(rows_ref, gain_ref, out_ref):
    rows = rows_ref[...].astype(F32)
    mean = jnp.mean(rows * rows, axis=-1, keepdims=True)
    out_ref[...] = (rows * lax.rsqrt(mean + 1e-06) * gain_ref[...]).astype(BF16)


def normed_rows(hidden, gain):
    rows, width = hidden.shape
    step = 64
    return pl.pallas_call(
        norm_kernel,
        grid=(rows // step,),
        in_specs=[
            pl.BlockSpec((step, width), lambda i: (i, 0)),
            pl.BlockSpec((width,), lambda i: (0,)),
        ],
        out_specs=pl.BlockSpec((step, width), lambda i: (i, 0)),
        out_shape=jax.ShapeDtypeStruct(hidden.shape, BF16),
        name="norm",
        cost_estimate=pl.CostEstimate(flops=2_000_000, bytes_accessed=2_400_000, transcendentals=128),
    )(hidden, gain)


def attended(scal, dy, q_ref, k_ref, v_ref, store):
    y, length = scal[3], scal[4]
    first = pl.multiple_of(lax.rem(y + dy, NY) * 128, 128)
    row = lax.broadcasted_iota(jnp.int32, (128, 512), 0) + first
    col = lax.broadcasted_iota(jnp.int32, (128, 512), 1)
    keep = (col <= row) & (col < length)
    for h in range(4):
        kv = slice((h // 2) * 128, (h // 2) * 128 + 128)
        score = lax.dot_general(
            q_ref[pl.ds(first, 128), h * 128 : h * 128 + 128],
            k_ref[:, kv],
            (((1,), (1,)), ((), ())),
            preferred_element_type=F32,
        )
        score = 50.0 * jnp.tanh(score * (1.0 / 50.0))
        score = jnp.where(keep, score, -1e30)
        top = jnp.max(score, axis=-1, keepdims=True)
        expo = jnp.exp(score - top)
        weights = (expo / jnp.sum(expo, axis=-1, keepdims=True)).astype(BF16)
        store(h, jnp.dot(weights, v_ref[:, kv], preferred_element_type=F32).astype(BF16))


def start(pairs, sem):
    for src, dst in pairs:
        half = src.shape[-1] // 2
        for part in range(2):
            cols = pl.ds(part * half, half)
            pltpu.make_async_copy(src.at[:, cols], dst.at[:, cols], sem).start()


def finished(target, rows, sem):
    part = target.at[pl.ds(0, rows)]
    pltpu.make_async_copy(part, part, sem).wait()


def rows_of(xbuf, y, dy, first, count):
    return xbuf.at[pl.ds(pl.multiple_of(lax.rem(y + dy, NY) * 128 + first, 64), count)]


def shards_of(ref, table, wbuf, base):
    for j in range(ref.shape[0]):
        yield ref.at[j], wbuf.at[pl.ds(pl.multiple_of(table[base + j], 8), 72)]


def fill_kernel(offsets, groups, n_old, scal, table, *refs):
    c, y = scal[2], scal[3]
    xs, refs = refs[: len(offsets)], refs[len(offsets) :]
    ws, refs = refs[: len(groups)], refs[len(groups) :]
    either, (xbuf, wbuf, sem) = refs[:-3][: -n_old or None], refs[-3:]

    start([(ref, rows_of(xbuf, y, *at, ref.shape[0])) for ref, at in zip(xs, offsets)], sem.at[0])
    for ref, group in zip(ws, groups):
        start(shards_of(ref, table, wbuf, group * 4), sem.at[1])
    if either:
        for core, ref, base in ((0, either[0], 28), (1, either[1], 60)):

            @pl.when(c == core)
            def _():
                start(shards_of(ref, table, wbuf, base), sem.at[1])

    if xs:
        finished(xbuf, sum(ref.shape[0] for ref in xs), sem.at[0])
    finished(wbuf, 72 * 4 * (len(groups) + bool(either)), sem.at[1])


VMEM = pl.BlockSpec(memory_space=pltpu.VMEM)
SMEM = pl.BlockSpec(memory_space=pltpu.SMEM)


def fill(scal, table, xs, offsets, ws, groups, either, held, width):
    operands = [scal, table, *xs, *ws, *either, *held]
    n = len(operands)
    return pl.pallas_call(
        functools.partial(fill_kernel, offsets, groups, len(held)),
        in_specs=[SMEM] * 2 + [ANY] * (n - 2 - len(held)) + [VMEM] * len(held),
        out_specs=[VMEM] * 2,
        out_shape=[pltpu.VMEM((512, width), BF16), pltpu.VMEM((width, 1536), BF16)],
        scratch_shapes=[pltpu.SemaphoreType.DMA((2,))],
        input_output_aliases={n - 2: 0, n - 1: 1} if held else {},
        compiler_params=pltpu.CompilerParams(vmem_limit_bytes=SMALL_LIMIT),
        cost_estimate=pl.CostEstimate(flops=0, bytes_accessed=18_000_000, transcendentals=0),
    )(*operands)


def turned(raw, cos_ref, sin_ref, first, count):
    rows = pl.ds(first, count)
    return raw * cos_ref[rows, :] + pltpu.roll(raw, 64, 1) * sin_ref[rows, :]


def queries(scal, dy, xbuf, wbuf, cos_ref, sin_ref, q, slot):
    first = pl.multiple_of(lax.rem(scal[3] + dy, NY) * 128, 128)
    raw = jnp.dot(xbuf[pl.ds(first, 128), :], wbuf[:, 0:512], preferred_element_type=F32)
    for h in range(4):
        one = turned(raw[:, h * 128 : h * 128 + 128], cos_ref, sin_ref, first, 128)
        q[pl.ds(slot * 128, 128), h * 128 : h * 128 + 128] = (one * 144.0 ** (-0.5)).astype(BF16)


def attended(scal, dy, q, slot, k_ref, v_ref, att):
    y, length = scal[3], scal[4]
    first = lax.rem(y + dy, NY) * 128
    row = lax.broadcasted_iota(jnp.int32, (128, 512), 0) + first
    col = lax.broadcasted_iota(jnp.int32, (128, 512), 1)
    keep = (col <= row) & (col < length)
    mine = pl.ds(slot * 128, 128)
    for h in range(4):
        kv = slice((h // 2) * 128, (h // 2) * 128 + 128)
        head = slice(h * 128, h * 128 + 128)
        score = lax.dot_general(
            q[mine, head], k_ref[:, kv], (((1,), (1,)), ((), ())), preferred_element_type=F32
        )
        score = 50.0 * jnp.tanh(score * (1.0 / 50.0))
        score = jnp.where(keep, score, -1e30)
        top = jnp.max(score, axis=-1, keepdims=True)
        expo = jnp.exp(score - top)
        weights = (expo / jnp.sum(expo, axis=-1, keepdims=True)).astype(BF16)
        att[mine, head] = jnp.dot(weights, v_ref[:, kv], preferred_element_type=F32).astype(BF16)


def project_kernel(
    scal, table, cos_ref, sin_ref, up_own, down_own, up_other, down_other, xbuf, old,
    k_out, v_out, far0, far1, wbuf, q, att, k_ref, v_ref, far, sem, osem,
):
    c, length = scal[2], scal[4]

    for core, halves, base in ((0, (up_other, down_other), 60), (1, (up_own, down_own), 28)):

        @pl.when(c == core)
        def _():
            for i, ref in enumerate(halves):
                start(shards_of(ref, table, wbuf, base + 2 * i), sem)

    finished(wbuf, 72 * 4, sem)
    live = lax.broadcasted_iota(jnp.int32, (512, 128), 0) < length
    raw = jnp.dot(xbuf[...], wbuf[:, 512:768], preferred_element_type=F32)
    for h in range(2):
        head = slice(h * 128, h * 128 + 128)
        k_ref[:, head] = jnp.where(live, turned(raw[:, head], cos_ref, sin_ref, 0, 512), 0.0).astype(BF16)
    start([(k_ref, k_out)], osem.at[0])
    raw = jnp.dot(xbuf[...], wbuf[:, 768:1024], preferred_element_type=F32)
    for h in range(2):
        head = slice(h * 128, h * 128 + 128)
        v_ref[:, head] = jnp.where(live, raw[:, head], 0.0).astype(BF16)
    start([(v_ref, v_out)], osem.at[1])
    queries(scal, 2, xbuf, wbuf, cos_ref, sin_ref, q, 0)
    attended(scal, 2, q, 0, k_ref, v_ref, att)
    chunk = 1152
    for at in range(0, wbuf.shape[0], chunk):
        cols = slice(at, at + chunk)
        far[:, cols] = lax.dot_general(
            att[...], wbuf[cols, 1024:1536], (((1,), (1,)), ((), ())), preferred_element_type=F32
        ).astype(BF16)
        for i, ref in enumerate((far0, far1)):
            cut = pl.ds(at, chunk)
            pltpu.make_async_copy(far.at[pl.ds(i * 64, 64), cut], ref.at[:, cut], osem.at[2 + i]).start()
    for i, (src, dst) in enumerate(((k_ref, k_out), (v_ref, v_out), (far.at[:64], far0), (far.at[64:], far1))):
        pltpu.make_async_copy(src, dst, osem.at[i]).wait()


def project(scal, table, cosine, sine, arrays, xbuf, wbuf):
    width = wbuf.shape[0]
    outs = [(512, 256), (512, 256), (64, width), (64, width)]
    n = 4 + len(arrays)
    return pl.pallas_call(
        project_kernel,
        in_specs=[SMEM] * 2 + [VMEM] * 2 + [ANY] * len(arrays) + [VMEM] * 2,
        out_specs=[ANY] * 4 + [VMEM],
        out_shape=[jax.ShapeDtypeStruct(shape, BF16) for shape in outs] + [pltpu.VMEM(wbuf.shape, BF16)],
        scratch_shapes=[
            pltpu.VMEM((128, 512), BF16),
            pltpu.VMEM((128, 512), BF16),
            pltpu.VMEM((512, 256), BF16),
            pltpu.VMEM((512, 256), BF16),
            pltpu.VMEM((128, width), BF16),
            pltpu.SemaphoreType.DMA,
            pltpu.SemaphoreType.DMA((4,)),
        ],
        input_output_aliases={n + 1: 4},
        compiler_params=pltpu.CompilerParams(vmem_limit_bytes=SMALL_LIMIT),
        name="project",
        cost_estimate=pl.CostEstimate(flops=4_000_000_000, bytes_accessed=10_000_000, transcendentals=524_288),
    )(scal, table, cosine, sine, *arrays, xbuf, wbuf)


def attend_kernel(blocks, outs, scal, cos_ref, sin_ref, k_ref, v_ref, xbuf, wbuf, *refs):
    out_refs, (q, att) = refs[:-2], refs[-2:]
    stride = blocks[-1] - blocks[0]

    def block(slot, carry):
        dy = blocks[0] + slot * stride
        queries(scal, dy, xbuf, wbuf, cos_ref, sin_ref, q, slot)
        attended(scal, dy, q, slot, k_ref, v_ref, att)
        return carry

    lax.fori_loop(0, len(blocks), block, 0)
    chunk = 1152

    def stretch(i, carry):
        at = pl.multiple_of(i * chunk, 128)
        partial = lax.dot_general(
            att[...], wbuf[pl.ds(at, chunk), 1024:1536], (((1,), (1,)), ((), ())), preferred_element_type=F32
        )
        for ref, first in zip(out_refs, outs):
            ref[:, pl.ds(at, chunk)] = partial[first : first + ref.shape[0]].astype(ref.dtype)
        return carry

    lax.fori_loop(0, wbuf.shape[0] // chunk, stretch, 0)


def attend(scal, cosine, sine, key, value, xbuf, wbuf, blocks, outs, count):
    width = wbuf.shape[0]
    n = len(blocks)
    return pl.pallas_call(
        functools.partial(attend_kernel, blocks, outs),
        in_specs=[SMEM] + [VMEM] * 6,
        out_specs=[VMEM] * len(outs),
        out_shape=[jax.ShapeDtypeStruct((count, width), BF16)] * len(outs),
        scratch_shapes=[pltpu.VMEM((n * 128, 512), BF16)] * 2,
        compiler_params=pltpu.CompilerParams(vmem_limit_bytes=SMALL_LIMIT),
        cost_estimate=pl.CostEstimate(
            flops=n * 1_400_000_000, bytes_accessed=1_000_000 + n * 1_200_000, transcendentals=n * 524_288
        ),
    )(scal, cosine, sine, key, value, xbuf, wbuf)


def finish_kernel(scal, rows_ref, own_ref, a1, b0, gain_ref, a0_hbm, b1_hbm, out_hbm, a0, b1, out, sem, osem):
    y, length = scal[3], scal[4]
    first = pltpu.make_async_copy(a0_hbm, a0, sem.at[0])
    second = pltpu.make_async_copy(b1_hbm, b1, sem.at[1])
    start([(a0_hbm, a0)], sem.at[0])
    start([(b1_hbm, b1)], sem.at[1])
    gain = gain_ref[...]
    count = 32
    for i in range(4):
        if i % 2 == 0:
            (first, second)[i // 2].wait()
        rows = slice(i * count, i * count + count)
        here = slice(i % 2 * count, i % 2 * count + count)
        before, after = ((a0, b0), (a1, b1))[i // 2]
        total = own_ref[rows, :].astype(F32) + before[here, :].astype(F32) + after[here, :].astype(F32)
        mean = jnp.mean(total * total, axis=-1, keepdims=True)
        post = total * lax.rsqrt(mean + 1e-06) * gain
        row = lax.broadcasted_iota(jnp.int32, (count, 1), 0) + y * 128 + i * count
        out[rows, :] = jnp.where(row < length, rows_ref[rows, :].astype(F32) + post, 0.0).astype(BF16)
        start([(out.at[rows], out_hbm.at[rows])], osem)
    pltpu.make_async_copy(out, out_hbm, osem).wait()


def finish(scal, hidden, own, a0, a1, b0, b1, gain):
    width = hidden.shape[-1]
    return pl.pallas_call(
        finish_kernel,
        in_specs=[SMEM] + [VMEM] * 5 + [ANY] * 2,
        out_specs=ANY,
        out_shape=jax.ShapeDtypeStruct(hidden.shape, BF16),
        scratch_shapes=[
            pltpu.VMEM((64, width), BF16),
            pltpu.VMEM((64, width), BF16),
            pltpu.VMEM(hidden.shape, BF16),
            pltpu.SemaphoreType.DMA((2,)),
            pltpu.SemaphoreType.DMA,
        ],
        compiler_params=pltpu.CompilerParams(vmem_limit_bytes=SMALL_LIMIT),
        name="finish",
        cost_estimate=pl.CostEstimate(flops=6_000_000, bytes_accessed=7_000_000, transcendentals=128),
    )(scal, hidden, own, a1, b0, gain, a0, b1)


def angle_tables(maxlen):
    half = HD // 2
    freqs = 10000.0 ** (-jnp.arange(half, dtype=F32) / half)
    angles = jnp.arange(maxlen, dtype=jnp.int32).astype(F32)[:, None] * freqs[None, :]
    cosine, sine = jnp.cos(angles), jnp.sin(angles)
    return jnp.concatenate([cosine, cosine], -1), jnp.concatenate([-sine, sine], -1)


def torus(array, d, cores=(0, 1)):
    pairs = [
        (spot(z, x, c), spot(z + d[c][0], x + d[c][1], c))
        for z in range(NZ)
        for x in range(NX)
        for c in cores
    ]
    return lax.ppermute(array, "dp", pairs)


def one_way(array, source):
    pairs = [(spot(z, x, source), spot(z, x, 1 - source)) for z in range(NZ) for x in range(NX)]
    return lax.ppermute(array, "dp", pairs)


def swapped(array):
    return plane(array, dc=1)


SMALL_UP, SMALL_DOWN = ((1, 0), (0, 1)), ((-1, 0), (0, -1))
LARGE_UP, LARGE_DOWN = ((0, 1), (1, 0)), ((0, -1), (-1, 0))
NEAR, FAR = (0, -1, 1, -2), (2, -3, 3, 4)


def wrapped(dz, dx):
    return dz % NZ, dx % NX


PLACES_A = tuple(
    tuple(wrapped(dz, dx) for dz in zs)
    for zs, dx in ((NEAR, 0), (NEAR, -1), (NEAR, 1), (FAR, -1), (FAR, 1), (FAR, -2), (NEAR, 2), (FAR, 0))
)
PLACES_B = tuple(
    tuple(wrapped(dz, dx) for dx in NEAR) for dz in (0, -1, 1, -2, 2, -3, 3, -4)
)


def row_table(z, x, core):
    places = jnp.array([PLACES_A, PLACES_B], jnp.int32)
    rows = []
    for dc in range(2):
        owner = (core + dc) % 2
        mine = jnp.where(owner == 0, places[0], places[1])
        rows.append((((z + mine[..., 0]) % NZ * NX + (x + mine[..., 1]) % NX) * 2 + owner) * 72)
    return jnp.stack(rows).reshape(-1).astype(jnp.int32)


def gathered_weights(shard, core, tables):
    first = core == 0
    s1 = torus(shard, SMALL_UP)
    s2 = torus(shard, SMALL_DOWN)
    s3 = torus(s1, SMALL_UP)
    s4 = torus(s2, SMALL_DOWN)
    s5 = torus(s3, SMALL_UP)
    s6 = torus(s4, SMALL_DOWN)
    s7 = torus(s6, SMALL_DOWN)
    near = jnp.stack([shard, s1, s2, s3])
    r1 = torus(near, LARGE_UP)
    r2 = torus(near, LARGE_DOWN)
    r2, tables = lax.optimization_barrier((r2, tables))
    far = jnp.stack([s4, s5, s6, s7])
    r3 = torus(jnp.where(first, far, r1), LARGE_UP)
    r4 = torus(jnp.where(first, far, r2), LARGE_DOWN)
    r5 = torus(r3, LARGE_UP)
    r6 = torus(jnp.where(first, *lax.optimization_barrier((r2, r4))), LARGE_DOWN)
    r7 = torus(r5[:2], LARGE_UP, (1,))
    r8 = torus(r6[2:], LARGE_DOWN, (1,))
    arrays = [near, r1, r2, r3, r4, r5, r6]
    others = [swapped(a) for a in arrays]
    far = far, one_way(far, 0)
    up = r7, one_way(r7, 1)
    down = r8, one_way(r8, 1)
    return arrays, others, far, up, down, tables


def layer(hidden, lengths, norm_gain, w_query, w_key, w_value, w_out, post_gain):
    _, local_len, width = hidden.shape
    hidden = hidden.reshape(local_len, width)
    place = lax.axis_index("dp")
    core = place % 2
    scal = jnp.stack([place // 8, (place // 2) % 4, core, lax.axis_index("mp"), lengths[0]]).astype(jnp.int32)
    shard = jnp.concatenate([w_query, w_key, w_value, w_out.T], axis=1)
    normed = normed_rows(hidden, norm_gain)
    above, below = column(normed, -1), column(normed, 1)
    across0 = column(above[:64], -1)
    across1 = column(below[64:], 1)
    tables = (scal, row_table(scal[0], scal[1], core), *angle_tables(local_len * NY))
    arrays, others, far, up, down, tables = gathered_weights(shard, core, tables)
    scal, table, cosine, sine = tables
    held = fill(
        scal, table, [normed, above, below], ((0, 0), (1, 0), (3, 0)), arrays[:5] + others[:3],
        (0, 1, 2, 3, 4, 8, 9, 10), far, (), width,
    )
    held = fill(
        scal, table, [across0, across1], ((2, 0), (2, 64)), arrays[5:] + others[3:5],
        (5, 6, 11, 12), (), held, width,
    )
    xbuf, wbuf = fill(scal, table, [], (), others[5:], (13, 14), (), held, width)
    rest = [up[0], down[0], up[1], down[1]]
    key, value, far0, far1, wbuf = project(scal, table, cosine, sine, rest, xbuf, wbuf)
    rfar0, rfar1 = column(far0, 1), column(far1, -1)
    up0, up1, down0, down1 = attend(scal, cosine, sine, key, value, xbuf, wbuf, (1, 3), (0, 64, 128, 192), 64)
    a1, b0 = column(up1, 1), column(down0, -1)
    (own,) = attend(scal, cosine, sine, key, value, xbuf, wbuf, (0,), (0,), 128)
    a0 = column((up0.astype(F32) + rfar0.astype(F32)).astype(BF16), 1)
    b1 = column((down1.astype(F32) + rfar1.astype(F32)).astype(BF16), -1)
    mixed = finish(scal, hidden, own, a0, a1, b0, b1, post_gain)
    return mixed[None], key[None], value[None]


def solution(mesh):
    return jax.shard_map(
        layer,
        mesh=mesh,
        in_specs=(
            P("dp", "mp", None),
            P("dp"),
            P(),
            P("dp", "mp"),
            P("dp", "mp"),
            P("dp", "mp"),
            P("mp", "dp"),
            P(),
        ),
        out_specs=(P("dp", "mp", None), P("dp", None, "mp"), P("dp", None, "mp")),
        check_vma=False,
    )
```
